128 devices in a mesh: row: 8 (over z, core), col: 16 (over x, y).
Axes of the slice: x: 4, y: 4, z: 4, core: 2. Of those that a mesh axis runs over, the one named last changes fastest.
Arguments:
- tile_values: float32 [2048, 512, 512], P(('row', 'col')), may hold values from -6 to 6
- tile_coords: int32 [2048, 2], P(('row', 'col')), may hold values from 0 to 3, as said below
- tile_counts: int32 [128], P(('row', 'col')), may hold values from 4 to 16, as said below
- restrict_basis: float32 [16384, 256], P(('row', 'col')), may hold values from -0.25 to 0.25
- prolong_basis: float32 [32768, 256], P(('col', 'row')), may hold values from -0.25 to 0.25
- row_partner: int32 [16, 8], replicated, may hold values from 0 to 7, as said below
- col_partner: int32 [8, 16], replicated, may hold values from 0 to 15, as said below
Outputs:
- coarse: float32 [4096, 8192], P('row', 'col')
The draws below stay inside these ranges and needn't reach their ends.
Inputs may be any that keep to these rules, and one draw needn't show every extreme that they name: `tile_coords`: within one device's 16 slots no two name the same (block row, block column); first entry below 4, second below 4; dead slots also hold such positions. `tile_counts`: number of leading slots of each device that are live; some device has all 16 live. `row_partner`: each row is a pairing: the partner of a part's partner is the part itself, never the part. `col_partner`: each row is a pairing: the partner of a part's partner is the part itself, never the part.
All inputs are finite; a program needn't handle non-finite values.
Results may differ from the reference program's by a relative error of at most 0.0003.
Values sent between devices are 32-bit elements; how exact they have to be, the bound alone decides.
A program may use at most 128 MiB of HBM per device.

```python
import jax
import jax.numpy as jnp
from jax import lax

TB = 512
K = 256
RB = 4
CB = 4
SLOTS = 16
FINE_ROWS = 16384
FINE_COLS = 32768
TILES = 2048
N_ROW = 8
N_COL = 16


def pairing(key, parts):
    order = jax.random.permutation(key, parts).astype(jnp.int32)
    swapped = order.reshape(-1, 2)[:, ::-1].reshape(-1)
    return jnp.zeros((parts,), jnp.int32).at[order].set(swapped)


def draw_row_partner(key, part):
    row_keys = jax.random.split(jax.random.fold_in(key, 11), N_COL)
    return jax.vmap(lambda one_key: pairing(one_key, N_ROW))(row_keys).astype(jnp.int32)


def draw_col_partner(key, part):
    col_keys = jax.random.split(jax.random.fold_in(key, 13), N_ROW)
    return jax.vmap(lambda one_key: pairing(one_key, N_COL))(col_keys).astype(jnp.int32)


def draw_tile_coords(key, part):
    devices_all = N_ROW * N_COL
    device_keys = jax.random.split(jax.random.fold_in(key, 17), devices_all)
    orders = jax.vmap(lambda one_key: jax.random.permutation(one_key, SLOTS))(device_keys).astype(jnp.int32)
    flat_orders = orders.reshape(-1)
    return jnp.stack([flat_orders // CB, flat_orders % CB], axis=1).astype(jnp.int32)


def draw_tile_counts(key, part):
    devices_all = N_ROW * N_COL
    lowest = max(1, SLOTS // 4)
    count_key = jax.random.fold_in(key, 19)
    drawn = jax.random.randint(count_key, (devices_all,), lowest, SLOTS + 1).astype(jnp.int32)
    chosen = jax.random.permutation(jax.random.fold_in(key, 23), devices_all).astype(jnp.int32)
    drawn = drawn.at[chosen[0]].set(SLOTS)
    return drawn.at[chosen[1]].set(lowest)


def level_of(stream_key, dims, pieces, smallest, largest):
    factor_of = 1.0
    for axis_at, shards_of in pieces:
        draws = jax.random.uniform(jax.random.fold_in(jax.random.fold_in(stream_key, 6), axis_at), (shards_of,), jnp.float32, smallest / len(pieces), largest / len(pieces))
        factor_of = factor_of * jnp.repeat(jnp.exp(draws), dims[axis_at] // shards_of).reshape((-1,) + (1,) * (len(dims) - 1 - axis_at))
    return factor_of


def normal_values(key, shape, deviation, most, shards=(), held_as=jnp.bfloat16):
    result = jax.random.normal(key, shape, jnp.float32) * deviation
    if len(shards) > 0:
        result = level_of(key, shape, shards, -0.22, 0.18) * result
    return jnp.clip(result, min=-most, max=most).astype(held_as)


def setup_inputs(seed: int = 0) -> dict:
    key_list = jax.random.split(jax.random.key(seed), 8)
    return {
        "tile_values": normal_values(key_list[0], (TILES, TB, TB), 1.0, 6.0, ((0, 128),), jnp.float32),
        "tile_coords": draw_tile_coords(jax.random.fold_in(key_list[7], 71), 0),
        "tile_counts": draw_tile_counts(jax.random.fold_in(key_list[7], 71), 0),
        "restrict_basis": normal_values(key_list[3], (FINE_ROWS, K), TB ** -0.5, 0.25, ((0, 128),), jnp.float32),
        "prolong_basis": normal_values(key_list[4], (FINE_COLS, K), TB ** -0.5, 0.25, ((0, 128),), jnp.float32),
        "row_partner": draw_row_partner(jax.random.fold_in(key_list[7], 71), 0),
        "col_partner": draw_col_partner(jax.random.fold_in(key_list[7], 71), 0),
    }


def device_grid(tile_block, coord_block, live_count, restrict_part, prolong_part):
    def add_slot(slot_index, grid_now):
        block_row = coord_block[slot_index, 0]
        block_col = coord_block[slot_index, 1]
        left = lax.dynamic_slice_in_dim(restrict_part, (block_row * TB).astype(jnp.int32), TB, 0)
        right = lax.dynamic_slice_in_dim(prolong_part, (block_col * TB).astype(jnp.int32), TB, 0)
        applied = jnp.dot(tile_block[slot_index], right, precision=lax.Precision.HIGHEST)
        product = jnp.dot(left.T, applied, precision=lax.Precision.HIGHEST)
        product = jnp.where(slot_index < live_count, product, jnp.zeros_like(product))
        place = ((block_row * K).astype(jnp.int32), (block_col * K).astype(jnp.int32))
        current = lax.dynamic_slice(grid_now, place, (K, K))
        return lax.dynamic_update_slice(grid_now, current + product, place)

    start_grid = jnp.zeros((RB * K, CB * K), jnp.float32)
    return lax.fori_loop(0, SLOTS, add_slot, start_grid)


def reference(tile_values, tile_coords, tile_counts, restrict_basis, prolong_basis, row_partner, col_partner):
    devices_all = N_ROW * N_COL
    tile_all = tile_values.reshape(devices_all, SLOTS, TB, TB)
    coord_all = tile_coords.reshape(devices_all, SLOTS, 2)
    restrict_all = restrict_basis.reshape(N_ROW, RB * TB, K)
    prolong_all = prolong_basis.reshape(N_COL, CB * TB, K)
    device_ids = jnp.arange(devices_all, dtype=jnp.int32)

    def one_device(inputs):
        tile_block, coord_block, live_count, device_id = inputs
        row_id = device_id // N_COL
        col_id = device_id % N_COL
        return device_grid(tile_block, coord_block, live_count, restrict_all[row_id], prolong_all[col_id])

    grids = lax.map(one_device, (tile_all, coord_all, tile_counts, device_ids))
    grids = grids.reshape(N_ROW, N_COL, RB * K, CB * K)
    row_ids = jnp.arange(N_ROW, dtype=jnp.int32)
    col_ids = jnp.arange(N_COL, dtype=jnp.int32)
    partner_rows = row_partner.T
    row_sum = grids + grids[partner_rows, col_ids[None, :]]
    row_halves = row_sum.reshape(N_ROW, N_COL, 2, RB * K // 2, CB * K)
    keep_row = row_ids[:, None] > partner_rows
    rowpair = jnp.where(keep_row[:, :, None, None], row_halves[:, :, 1], row_halves[:, :, 0])
    col_sum = rowpair + rowpair[row_ids[:, None], col_partner]
    col_halves = col_sum.reshape(N_ROW, N_COL, RB * K // 2, 2, CB * K // 2)
    keep_col = col_ids[None, :] > col_partner
    quarter = jnp.where(keep_col[:, :, None, None], col_halves[:, :, :, 1], col_halves[:, :, :, 0])
    return quarter.transpose(0, 2, 1, 3).reshape(N_ROW * RB * K // 2, N_COL * CB * K // 2)
```

```python
import jax
import jax.numpy as jnp
from jax import lax
from jax.experimental import pallas as pl
from jax.experimental.pallas import tpu as pltpu
from jax.sharding import PartitionSpec as P

MESH = pl.DeviceIdType.MESH
HIGH = lax.Precision.HIGH

TB = 512
K = 256
RB = 4
CB = 4
SLOTS = 16
N_ROW = 8
N_COL = 16
CH = 4
SL = K // N_ROW

Z_PEERS = ((1, 0), (3, 0), (2, 0), (1, 1), (3, 1), (2, 1), (0, 1))
XY_PEERS = tuple(
    sorted(
        ((dx, dy) for dx in range(4) for dy in range(4) if dx or dy),
        key=lambda d: (min(d[0], 4 - d[0]) + min(d[1], 4 - d[1]), d),
    )
)


def kernel(
    tiles_hbm,
    q_ref,
    p_hbm,
    coords,
    counts,
    row_partner,
    col_partner,
    out_ref,
    tiles,
    pbuf,
    qt,
    ubuf,
    gv,
    kept,
    recv1_0,
    recv1_1,
    recv1_2,
    recv1_3,
    snd2,
    inc,
    cs,
    crecv_0,
    crecv_1,
    csnd2,
    cinc,
    slot_sm,
    live_sm,
    tile_sem,
    own_sem,
    p_send,
    p_fsend,
    p_recv,
    q_send,
    q_recv,
    s1_send,
    s1_recv,
    s2_send,
    s2_recv,
    x1_send,
    x1_recv,
    x2_send,
    x2_recv,
):
    recv1 = (recv1_0, recv1_1, recv1_2, recv1_3)
    crecv = (crecv_0, crecv_1)
    r = lax.axis_index("row")
    c = lax.axis_index("col")
    z, core = r // 2, r % 2
    x, y = c // 4, c % 4

    tile_cp = pltpu.make_async_copy(tiles_hbm, tiles, tile_sem)
    tile_cp.start()
    own_cp = pltpu.make_async_copy(p_hbm, pbuf.at[z, core], own_sem)
    own_cp.start()

    z_peers = [((z + dz) % 4) * 2 + (core + dc) % 2 for dz, dc in Z_PEERS]
    xy_peers = [((x + dx) % 4) * 4 + (y + dy) % 4 for dx, dy in XY_PEERS]

    barrier = pltpu.get_barrier_semaphore()
    for peer in z_peers:
        pl.semaphore_signal(barrier, inc=1, device_id={"row": peer}, device_id_type=MESH)
    for peer in xy_peers:
        pl.semaphore_signal(barrier, inc=1, device_id={"col": peer}, device_id_type=MESH)

    qt[x, y] = q_ref[...].T

    for pos in range(RB * CB):
        slot = jnp.int32(0)
        for s in range(SLOTS):
            hit = coords[s, 0] * CB + coords[s, 1] == pos
            slot = jnp.where(hit, jnp.int32(s), slot)
        slot_sm[pos] = slot
        live_sm[pos] = jnp.where(slot < counts[0], jnp.int32(1), jnp.int32(0))

    pl.semaphore_wait(barrier, len(z_peers) + len(xy_peers))

    sibling = z * 2 + (1 - core)
    p_cps = []
    for n, dz in enumerate((1, 3, 2)):
        cp = pltpu.make_async_remote_copy(
            src_ref=p_hbm,
            dst_ref=pbuf.at[z, core],
            send_sem=p_send.at[n],
            recv_sem=p_recv.at[z, core],
            device_id={"row": ((z + dz) % 4) * 2 + core},
            device_id_type=MESH,
        )
        cp.start()
        p_cps.append(cp)
    cp = pltpu.make_async_remote_copy(
        src_ref=p_hbm,
        dst_ref=pbuf.at[z, core],
        send_sem=p_send.at[3],
        recv_sem=p_recv.at[z, core],
        device_id={"row": sibling},
        device_id_type=MESH,
    )
    cp.start()
    p_cps.append(cp)

    def q_copy(ref, n, recv, dest):
        return pltpu.make_async_remote_copy(
            src_ref=ref,
            dst_ref=ref,
            send_sem=q_send.at[n],
            recv_sem=recv,
            device_id={"col": dest},
            device_id_type=MESH,
        )

    half = K // 2
    q_cps = []
    for n, d in enumerate((1, 3, 2)):
        cp = q_copy(qt.at[x, y, pl.ds(0, half)], n, q_recv.at[0, x], ((x + d) % 4) * 4 + y)
        cp.start()
        q_cps.append(cp)
        cp = q_copy(qt.at[x, y, pl.ds(half, half)], 3 + n, q_recv.at[1, y], x * 4 + (y + d) % 4)
        cp.start()
        q_cps.append(cp)
    for d in (1, 3, 2):
        xs, ys = (x + d) % 4, (y + d) % 4
        q_copy(qt.at[xs, y, pl.ds(0, half)], 0, q_recv.at[0, xs], c).wait_recv()
        q_copy(qt.at[x, ys, pl.ds(half, half)], 0, q_recv.at[1, ys], c).wait_recv()
    for n, d in enumerate((1, 3, 2)):
        cp = q_copy(qt.at[:, y, pl.ds(0, half)], 6 + n, q_recv.at[2, y], x * 4 + (y + d) % 4)
        cp.start()
        q_cps.append(cp)
        cp = q_copy(qt.at[x, :, pl.ds(half, half)], 9 + n, q_recv.at[3, x], ((x + d) % 4) * 4 + y)
        cp.start()
        q_cps.append(cp)

    def p_wait(zs, cs_):
        pltpu.make_async_copy(pbuf.at[zs, cs_], pbuf.at[zs, cs_], p_recv.at[zs, cs_]).wait()

    def p_forward(n, zs):
        cp = pltpu.make_async_remote_copy(
            src_ref=pbuf.at[zs, core],
            dst_ref=pbuf.at[zs, core],
            send_sem=p_fsend.at[n],
            recv_sem=p_recv.at[zs, core],
            device_id={"row": sibling},
            device_id_type=MESH,
        )
        cp.start()
        p_cps.append(cp)

    def apply_block(b):
        def one(a, carry):
            right = pbuf[b].reshape(TB, K)
            pos = a * CB + b
            tile = tiles[slot_sm[pos]]
            ubuf[pos] = jnp.dot(tile, right, precision=HIGH, preferred_element_type=jnp.float32)
            return carry

        lax.fori_loop(0, RB, one, 0)

    own_cp.wait()
    p_wait(z, 1 - core)
    tile_cp.wait()
    apply_block(z)
    for n, d in enumerate((1, 3)):
        zs = (z + d) % 4
        p_wait(zs, core)
        p_forward(n, zs)
    for d in (1, 3):
        zs = (z + d) % 4
        p_wait(zs, 1 - core)
        apply_block(zs)
    zs = (z + 2) % 4
    p_wait(zs, core)
    p_forward(2, zs)
    p_wait(zs, 1 - core)
    apply_block(zs)

    for d in (1, 3, 2):
        xs, ys = (x + d) % 4, (y + d) % 4
        q_copy(qt.at[:, ys, pl.ds(0, half)], 0, q_recv.at[2, ys], c).wait_recv()
        q_copy(qt.at[xs, :, pl.ds(half, half)], 0, q_recv.at[3, xs], c).wait_recv()

    my_rp = row_partner[c, r]
    my_cp = col_partner[r, c]
    my_h = jnp.where(r > my_rp, jnp.int32(1), jnp.int32(0))
    my_g = jnp.where(c > my_cp, jnp.int32(1), jnp.int32(0))
    partner_g = jnp.where(c > col_partner[my_rp, c], jnp.int32(1), jnp.int32(0))

    def blocks(dst, ch, row_half, keep_col):
        a = 2 * row_half + ch % 2
        col_half = (1 - keep_col) if ch < 2 else keep_col

        def one(n, carry):
            pos = a * CB + 2 * col_half + n
            left = jnp.concatenate([qt[a, i] for i in range(4)], axis=1)
            g = jnp.dot(left, ubuf[pos], precision=HIGH, preferred_element_type=jnp.float32)
            g = jnp.where(live_sm[pos] > 0, g, jnp.zeros_like(g))
            dst[ch, :, n] = g.reshape(N_ROW, SL, K)
            return carry

        lax.fori_loop(0, 2, one, 0)

    def send1(ch):
        recv1[ch][r] = gv[ch, r]
        for peer in z_peers:
            pltpu.make_async_remote_copy(
                src_ref=gv.at[ch, peer],
                dst_ref=recv1[ch].at[r],
                send_sem=s1_send.at[ch],
                recv_sem=s1_recv.at[ch],
                device_id={"row": peer},
                device_id_type=MESH,
            ).start()

    def take(ref, n, sem):
        view = ref.at[pl.ds(0, n)]
        pltpu.make_async_copy(view, view, sem).wait()

    def send2(ch):
        take(recv1[ch], N_ROW - 1, s1_recv.at[ch])

        def one(k, carry):
            snd2[ch, k] = recv1[ch][row_partner[c, k]]
            return carry

        lax.fori_loop(0, N_ROW, one, 0)
        inc[ch, r] = snd2[ch, r]
        for peer in z_peers:
            pltpu.make_async_remote_copy(
                src_ref=snd2.at[ch, peer],
                dst_ref=inc.at[ch, r],
                send_sem=s2_send.at[ch],
                recv_sem=s2_recv.at[ch],
                device_id={"row": peer},
                device_id_type=MESH,
            ).start()

    def cross1(ch):
        take(inc.at[ch], N_ROW - 1, s2_recv.at[ch])
        cs[ch] = (kept[ch] + inc[ch]).reshape(N_COL, SL, K)
        crecv[ch][c] = cs[ch, c]
        for peer in xy_peers:
            pltpu.make_async_remote_copy(
                src_ref=cs.at[ch, peer],
                dst_ref=crecv[ch].at[c],
                send_sem=x1_send.at[ch],
                recv_sem=x1_recv.at[ch],
                device_id={"col": peer},
                device_id_type=MESH,
            ).start()

    def cross2(ch):
        take(crecv[ch], N_COL - 1, x1_recv.at[ch])

        def one(k, carry):
            csnd2[ch, k] = crecv[ch][col_partner[r, k]]
            return carry

        lax.fori_loop(0, N_COL, one, 0)
        cinc[ch, c] = csnd2[ch, c]
        for peer in xy_peers:
            pltpu.make_async_remote_copy(
                src_ref=csnd2.at[ch, peer],
                dst_ref=cinc.at[ch, c],
                send_sem=x2_send.at[ch],
                recv_sem=x2_recv.at[ch],
                device_id={"col": peer},
                device_id_type=MESH,
            ).start()

    def finish(a):
        take(inc.at[2 + a], N_ROW - 1, s2_recv.at[2 + a])
        take(cinc.at[a], N_COL - 1, x2_recv.at[a])
        for n in range(2):
            total = kept[2 + a, :, n] + inc[2 + a, :, n]
            total = total + cinc[a].reshape(N_ROW, 2, SL, K)[:, n]
            out_ref[a * K : (a + 1) * K, n * K : (n + 1) * K] = total.reshape(K, K)

    given_h = 1 - my_h
    blocks(gv, 0, given_h, partner_g)
    send1(0)
    blocks(gv, 1, given_h, partner_g)
    send1(1)
    blocks(gv, 2, given_h, partner_g)
    blocks(gv, 3, given_h, partner_g)
    for ch in range(CH):
        blocks(kept, ch, my_h, my_g)
    send2(0)
    send2(1)
    send1(2)
    send1(3)
    cross1(0)
    cross1(1)
    cross2(0)
    send2(2)
    cross2(1)
    send2(3)
    finish(0)
    finish(1)

    for cp in p_cps + q_cps:
        cp.wait_send()
    for ch in range(CH):
        take(gv.at[ch], N_ROW - 1, s1_send.at[ch])
        take(snd2.at[ch], N_ROW - 1, s2_send.at[ch])
    for ch in range(2):
        take(cs.at[ch], N_COL - 1, x1_send.at[ch])
        take(csnd2.at[ch], N_COL - 1, x2_send.at[ch])


def body(tile_values, tile_coords, tile_counts, restrict_basis, prolong_basis, row_partner, col_partner):
    f32 = jnp.float32
    dma = pltpu.SemaphoreType.DMA
    any_spec = pl.BlockSpec(memory_space=pl.ANY)
    vmem_spec = pl.BlockSpec(memory_space=pltpu.VMEM)
    smem_spec = pl.BlockSpec(memory_space=pltpu.SMEM)
    return pl.pallas_call(
        kernel,
        out_shape=jax.ShapeDtypeStruct((RB * K // 2, CB * K // 2), f32),
        in_specs=[any_spec, vmem_spec, any_spec, smem_spec, smem_spec, smem_spec, smem_spec],
        out_specs=vmem_spec,
        scratch_shapes=[
            pltpu.VMEM((SLOTS, TB, TB), f32),
            pltpu.VMEM((4, 2, TB // 2, K), f32),
            pltpu.VMEM((4, 4, K, TB // 4), f32),
            pltpu.VMEM((RB * CB, TB, K), f32),
            pltpu.VMEM((CH, N_ROW, 2, SL, K), f32),
            pltpu.VMEM((CH, N_ROW, 2, SL, K), f32),
            *[pltpu.VMEM((N_ROW, 2, SL, K), f32)] * CH,
            pltpu.VMEM((CH, N_ROW, 2, SL, K), f32),
            pltpu.VMEM((CH, N_ROW, 2, SL, K), f32),
            pltpu.VMEM((2, N_COL, SL, K), f32),
            *[pltpu.VMEM((N_COL, SL, K), f32)] * 2,
            pltpu.VMEM((2, N_COL, SL, K), f32),
            pltpu.VMEM((2, N_COL, SL, K), f32),
            pltpu.SMEM((RB * CB,), jnp.int32),
            pltpu.SMEM((RB * CB,), jnp.int32),
            dma,
            dma,
            dma((4,)),
            dma((3,)),
            dma((4, 2)),
            dma((12,)),
            dma((4, 4)),
            dma((CH,)),
            dma((CH,)),
            dma((CH,)),
            dma((CH,)),
            dma((2,)),
            dma((2,)),
            dma((2,)),
            dma((2,)),
        ],
        compiler_params=pltpu.CompilerParams(collective_id=0, has_side_effects=True, vmem_limit_bytes=60 << 20),
    )(tile_values, restrict_basis, prolong_basis, tile_coords, tile_counts, row_partner, col_partner)


def solution(mesh):
    in_specs = (
        P(("row", "col"), None, None),
        P(("row", "col"), None),
        P(("row", "col")),
        P(("row", "col"), None),
        P(("col", "row"), None),
        P(),
        P(),
    )
    return jax.shard_map(body, mesh=mesh, in_specs=in_specs, out_specs=P("row", "col"), check_vma=False)
```

```python
import jax
import jax.numpy as jnp
from jax import lax
from jax.experimental import pallas as pl
from jax.experimental.pallas import tpu as pltpu
from jax.sharding import PartitionSpec as P

MESH = pl.DeviceIdType.MESH
HIGH = lax.Precision.HIGH

TB = 512
K = 256
RB = 4
CB = 4
SLOTS = 16
N_ROW = 8
N_COL = 16
CH = 4
SL = K // N_ROW

Z_PEERS = ((1, 0), (3, 0), (2, 0), (1, 1), (3, 1), (2, 1), (0, 1))
XY_PEERS = tuple(
    sorted(
        ((dx, dy) for dx in range(4) for dy in range(4) if dx or dy),
        key=lambda d: (min(d[0], 4 - d[0]) + min(d[1], 4 - d[1]), d),
    )
)


def kernel(
    tiles_hbm,
    q_hbm,
    p_hbm,
    coords,
    counts,
    row_partner,
    col_partner,
    out_ref,
    tiles,
    qin,
    pbuf,
    qt,
    ubuf,
    gv,
    kept,
    recv1_0,
    recv1_1,
    recv1_2,
    recv1_3,
    snd2,
    inc,
    cs,
    crecv_0,
    crecv_1,
    csnd2,
    cinc,
    slot_sm,
    live_sm,
    tile_sem,
    own_sem,
    q_own_sem,
    p_send,
    p_recv,
    q_send,
    q1_recv,
    q2_recv,
    q3_recv,
    s1_send,
    s1_recv,
    s2_send,
    s2_recv,
    x1_send,
    x1_recv,
    x2_send,
    x2_recv,
):
    recv1 = (recv1_0, recv1_1, recv1_2, recv1_3)
    crecv = (crecv_0, crecv_1)
    r = lax.axis_index("row")
    c = lax.axis_index("col")
    z, core = r // 2, r % 2
    x, y = c // 4, c % 4

    z_peers = [((z + dz) % 4) * 2 + (core + dc) % 2 for dz, dc in Z_PEERS]
    xy_peers = [((x + dx) % 4) * 4 + (y + dy) % 4 for dx, dy in XY_PEERS]

    barrier = pltpu.get_barrier_semaphore()
    for peer in z_peers:
        pl.semaphore_signal(barrier, inc=1, device_id={"row": peer}, device_id_type=MESH)
    for peer in xy_peers:
        pl.semaphore_signal(barrier, inc=1, device_id={"col": peer}, device_id_type=MESH)

    own_cp = pltpu.make_async_copy(p_hbm, pbuf.at[z, core], own_sem)
    own_cp.start()
    q_cp = pltpu.make_async_copy(q_hbm, qin, q_own_sem)
    q_cp.start()
    tile_cp = pltpu.make_async_copy(tiles_hbm, tiles, tile_sem)
    tile_cp.start()

    q_cp.wait()
    qt[x, y] = qin[...].T
    own_cp.wait()

    def find_slot(pos, carry):
        slot = jnp.int32(0)
        for s in range(SLOTS):
            hit = coords[0, s] * CB + coords[1, s] == pos
            slot = jnp.where(hit, jnp.int32(s), slot)
        slot_sm[pos] = slot
        live_sm[pos] = jnp.where(slot < counts[0], jnp.int32(1), jnp.int32(0))
        return carry

    pl.semaphore_wait(barrier, len(z_peers) + len(xy_peers))

    up, down, far = lambda v: (v + 1) % 4, lambda v: (v + 3) % 4, lambda v: (v + 2) % 4
    hb = TB // 4
    sibling = z * 2 + (1 - core)

    p_cps = []

    def p_half(zs, cs_, h):
        return pbuf.at[zs, cs_, pl.ds(h * hb, hb)]

    def p_send_to(zs, h, row):
        n = len(p_cps)
        cp = pltpu.make_async_remote_copy(
            src_ref=p_half(zs, core, h),
            dst_ref=p_half(zs, core, h),
            send_sem=p_send.at[n],
            recv_sem=p_recv.at[zs, core, h],
            device_id={"row": row},
            device_id_type=MESH,
        )
        cp.start()
        p_cps.append(cp)

    def p_wait(zs, cs_, h):
        view = p_half(zs, cs_, h)
        pltpu.make_async_copy(view, view, p_recv.at[zs, cs_, h]).wait()

    z_up, z_down = up(z) * 2 + core, down(z) * 2 + core

    q_cps = []

    def q_ref_of(kind, i, j, lo, n):
        xs, ys = (i, j) if kind == 0 else (j, i)
        return qt.at[xs, ys, pl.ds(kind * 128 + lo, n)]

    me_i, me_j = (x, y), (y, x)

    def q_dest(kind, i, j):
        return i * 4 + j if kind == 0 else j * 4 + i

    def q_send_to(kind, i, j, lo, n, sem, dest):
        cp = pltpu.make_async_remote_copy(
            src_ref=q_ref_of(kind, i, j, lo, n),
            dst_ref=q_ref_of(kind, i, j, lo, n),
            send_sem=q_send.at[len(q_cps)],
            recv_sem=sem,
            device_id={"col": dest},
            device_id_type=MESH,
        )
        cp.start()
        q_cps.append(cp)

    def q_wait(kind, i, j, lo, n, sem):
        view = q_ref_of(kind, i, j, lo, n)
        pltpu.make_async_copy(view, view, sem).wait()

    def q_first(kind):
        i, j = me_i[kind], me_j[kind]
        for step in (up, down, far):
            q_send_to(kind, i, j, 0, 128, q1_recv.at[kind, i], q_dest(kind, step(i), j))

    def q_second(kind, i):
        mi, j = me_i[kind], me_j[kind]
        for step in (up, down):
            q_send_to(kind, i, j, 0, 128, q2_recv.at[kind, i, j], q_dest(kind, mi, step(j)))

    def q_take1(kind, step):
        i, j = step(me_i[kind]), me_j[kind]
        q_wait(kind, i, j, 0, 128, q1_recv.at[kind, i])
        q_second(kind, i)

    def q_take2(kind, i):
        mi, j = me_i[kind], me_j[kind]
        q_wait(kind, i, down(j), 0, 128, q2_recv.at[kind, i, down(j)])
        q_send_to(kind, i, down(j), 0, 64, q3_recv.at[kind, i, 0], q_dest(kind, mi, up(j)))
        q_wait(kind, i, up(j), 0, 128, q2_recv.at[kind, i, up(j)])
        q_send_to(kind, i, up(j), 64, 64, q3_recv.at[kind, i, 1], q_dest(kind, mi, down(j)))

    def q_take3(kind, i):
        j = far(me_j[kind])
        q_wait(kind, i, j, 0, 64, q3_recv.at[kind, i, 0])
        q_wait(kind, i, j, 64, 64, q3_recv.at[kind, i, 1])

    def apply_block(b):
        def one(a, carry):
            right = pbuf[b].reshape(TB, K)
            pos = a * CB + b
            tile = tiles[slot_sm[pos]]
            ubuf[pos] = jnp.dot(tile, right, precision=HIGH, preferred_element_type=jnp.float32)
            return carry

        lax.fori_loop(0, RB, one, 0)

    def apply_half(b, cs_, first):
        def one(a, carry):
            pos = a * CB + b
            cols = pl.ds(pl.multiple_of(cs_ * (TB // 2), TB // 2), TB // 2)
            tile = tiles[slot_sm[pos], :, cols]
            u = jnp.dot(tile, pbuf[b, cs_], precision=HIGH, preferred_element_type=jnp.float32)
            ubuf[pos] = u if first else ubuf[pos] + u
            return carry

        lax.fori_loop(0, RB, one, 0)

    for h in (0, 1):
        p_send_to(z, h, z_up)
        p_send_to(z, 1 - h, z_down)
    for kind in (0, 1):
        q_first(kind)
    for h in (0, 1):
        p_send_to(z, h, sibling)
    for kind in (0, 1):
        q_second(kind, me_i[kind])
    lax.fori_loop(0, RB * CB, find_slot, 0)
    for step in (up, down):
        for kind in (0, 1):
            q_take1(kind, step)
    for h in (0, 1):
        p_wait(z, 1 - core, h)
    tile_cp.wait()
    for kind in (0, 1):
        q_take1(kind, far)
    p_wait(down(z), core, 0)
    p_send_to(down(z), 0, z_up)
    p_wait(up(z), core, 1)
    p_send_to(up(z), 1, z_down)
    p_send_to(down(z), 0, sibling)
    p_send_to(up(z), 1, sibling)
    apply_block(z)
    for kind in (0, 1):
        q_take2(kind, me_i[kind])
    p_wait(down(z), core, 1)
    p_send_to(down(z), 1, sibling)
    p_wait(up(z), core, 0)
    p_send_to(up(z), 0, sibling)
    for step in (up, down):
        for kind in (0, 1):
            q_take2(kind, step(me_i[kind]))
    for h in (0, 1):
        p_wait(down(z), 1 - core, h)
    apply_block(down(z))
    for kind in (0, 1):
        q_take2(kind, far(me_i[kind]))
    for h in (0, 1):
        p_wait(far(z), core, h)
        p_send_to(far(z), h, sibling)
    for h in (0, 1):
        p_wait(up(z), 1 - core, h)
    apply_block(up(z))
    apply_half(far(z), core, True)
    for h in (0, 1):
        p_wait(far(z), 1 - core, h)
    apply_half(far(z), 1 - core, False)
    for kind in (0, 1):
        for step in (lambda v: v, up, down, far):
            q_take3(kind, step(me_i[kind]))

    my_rp = row_partner[r, c]
    my_cp = col_partner[r, c]
    my_h = jnp.where(r > my_rp, jnp.int32(1), jnp.int32(0))
    my_g = jnp.where(c > my_cp, jnp.int32(1), jnp.int32(0))
    partner_g = jnp.where(c > col_partner[my_rp, c], jnp.int32(1), jnp.int32(0))

    def blocks(dst, ch, row_half, keep_col):
        a = 2 * row_half + ch % 2
        col_half = (1 - keep_col) if ch < 2 else keep_col

        pos = a * CB + 2 * col_half
        left = jnp.concatenate([qt[a, i] for i in range(4)], axis=1)
        right = jnp.concatenate([ubuf[pos], ubuf[pos + 1]], axis=1)
        g = jnp.dot(left, right, precision=HIGH, preferred_element_type=jnp.float32)
        for n in range(2):
            gn = g[:, n * K : (n + 1) * K]
            gn = jnp.where(live_sm[pos + n] > 0, gn, jnp.zeros_like(gn))
            dst[ch, :, n] = gn.reshape(N_ROW, SL, K)

    def send1(ch):
        recv1[ch][r] = gv[ch, r]
        for peer in z_peers:
            pltpu.make_async_remote_copy(
                src_ref=gv.at[ch, peer],
                dst_ref=recv1[ch].at[r],
                send_sem=s1_send.at[ch],
                recv_sem=s1_recv.at[ch],
                device_id={"row": peer},
                device_id_type=MESH,
            ).start()

    def take(ref, n, sem):
        view = ref.at[pl.ds(0, n)]
        pltpu.make_async_copy(view, view, sem).wait()

    def send2(ch):
        take(recv1[ch], N_ROW - 1, s1_recv.at[ch])

        def one(k, carry):
            snd2[ch, k] = recv1[ch][row_partner[k, c]]
            return carry

        lax.fori_loop(0, N_ROW, one, 0)
        inc[ch, r] = snd2[ch, r]
        for peer in z_peers:
            pltpu.make_async_remote_copy(
                src_ref=snd2.at[ch, peer],
                dst_ref=inc.at[ch, r],
                send_sem=s2_send.at[ch],
                recv_sem=s2_recv.at[ch],
                device_id={"row": peer},
                device_id_type=MESH,
            ).start()

    def cross1(ch):
        take(inc.at[ch], N_ROW - 1, s2_recv.at[ch])
        cs[ch] = (kept[ch] + inc[ch]).reshape(N_COL, SL, K)
        crecv[ch][c] = cs[ch, c]
        for peer in xy_peers:
            pltpu.make_async_remote_copy(
                src_ref=cs.at[ch, peer],
                dst_ref=crecv[ch].at[c],
                send_sem=x1_send.at[ch],
                recv_sem=x1_recv.at[ch],
                device_id={"col": peer},
                device_id_type=MESH,
            ).start()

    def cross2(ch):
        take(crecv[ch], N_COL - 1, x1_recv.at[ch])

        def one(k, carry):
            csnd2[ch, k] = crecv[ch][col_partner[r, k]]
            return carry

        lax.fori_loop(0, N_COL, one, 0)
        cinc[ch, c] = csnd2[ch, c]
        for peer in xy_peers:
            pltpu.make_async_remote_copy(
                src_ref=csnd2.at[ch, peer],
                dst_ref=cinc.at[ch, c],
                send_sem=x2_send.at[ch],
                recv_sem=x2_recv.at[ch],
                device_id={"col": peer},
                device_id_type=MESH,
            ).start()

    def finish(a):
        take(inc.at[2 + a], N_ROW - 1, s2_recv.at[2 + a])
        take(cinc.at[a], N_COL - 1, x2_recv.at[a])
        for n in range(2):
            total = kept[2 + a, :, n] + inc[2 + a, :, n]
            total = total + cinc[a].reshape(N_ROW, 2, SL, K)[:, n]
            out_ref[a * K : (a + 1) * K, n * K : (n + 1) * K] = total.reshape(K, K)

    given_h = 1 - my_h
    blocks(gv, 0, given_h, partner_g)
    send1(0)
    blocks(gv, 1, given_h, partner_g)
    send1(1)
    blocks(gv, 2, given_h, partner_g)
    blocks(gv, 3, given_h, partner_g)
    for ch in range(CH):
        blocks(kept, ch, my_h, my_g)
    send2(0)
    send2(1)
    send1(2)
    send1(3)
    cross1(0)
    cross1(1)
    cross2(0)
    send2(2)
    cross2(1)
    send2(3)
    finish(0)
    finish(1)

    for cp in p_cps + q_cps:
        cp.wait_send()
    for ch in range(CH):
        take(gv.at[ch], N_ROW - 1, s1_send.at[ch])
        take(snd2.at[ch], N_ROW - 1, s2_send.at[ch])
    for ch in range(2):
        take(cs.at[ch], N_COL - 1, x1_send.at[ch])
        take(csnd2.at[ch], N_COL - 1, x2_send.at[ch])


def body(tile_values, tile_coords, tile_counts, restrict_basis, prolong_basis, row_partner, col_partner):
    f32 = jnp.float32
    dma = pltpu.SemaphoreType.DMA
    any_spec = pl.BlockSpec(memory_space=pl.ANY)
    vmem_spec = pl.BlockSpec(memory_space=pltpu.VMEM)
    smem_spec = pl.BlockSpec(memory_space=pltpu.SMEM)
    return pl.pallas_call(
        kernel,
        out_shape=jax.ShapeDtypeStruct((RB * K // 2, CB * K // 2), f32),
        in_specs=[any_spec, any_spec, any_spec, smem_spec, smem_spec, smem_spec, smem_spec],
        out_specs=vmem_spec,
        scratch_shapes=[
            pltpu.VMEM((SLOTS, TB, TB), f32),
            pltpu.VMEM((TB // 4, K), f32),
            pltpu.VMEM((4, 2, TB // 2, K), f32),
            pltpu.VMEM((4, 4, K, TB // 4), f32),
            pltpu.VMEM((RB * CB, TB, K), f32),
            pltpu.VMEM((CH, N_ROW, 2, SL, K), f32),
            pltpu.VMEM((CH, N_ROW, 2, SL, K), f32),
            *[pltpu.VMEM((N_ROW, 2, SL, K), f32)] * CH,
            pltpu.VMEM((CH, N_ROW, 2, SL, K), f32),
            pltpu.VMEM((CH, N_ROW, 2, SL, K), f32),
            pltpu.VMEM((2, N_COL, SL, K), f32),
            *[pltpu.VMEM((N_COL, SL, K), f32)] * 2,
            pltpu.VMEM((2, N_COL, SL, K), f32),
            pltpu.VMEM((2, N_COL, SL, K), f32),
            pltpu.SMEM((RB * CB,), jnp.int32),
            pltpu.SMEM((RB * CB,), jnp.int32),
            dma,
            dma,
            dma,
            dma((14,)),
            dma((4, 2, 2)),
            dma((38,)),
            dma((2, 4)),
            dma((2, 4, 4)),
            dma((2, 4, 2)),
            dma((CH,)),
            dma((CH,)),
            dma((CH,)),
            dma((CH,)),
            dma((2,)),
            dma((2,)),
            dma((2,)),
            dma((2,)),
        ],
        compiler_params=pltpu.CompilerParams(collective_id=0, has_side_effects=True, vmem_limit_bytes=60 << 20),
    )(tile_values, restrict_basis, prolong_basis, tile_coords.T, tile_counts, row_partner.T, col_partner)


def solution(mesh):
    in_specs = (
        P(("row", "col"), None, None),
        P(("row", "col"), None),
        P(("row", "col")),
        P(("row", "col"), None),
        P(("col", "row"), None),
        P(),
        P(),
    )
    return jax.shard_map(body, mesh=mesh, in_specs=in_specs, out_specs=P("row", "col"), check_vma=False)
```

```python
import jax
import jax.numpy as jnp
from jax import lax
from jax.experimental import pallas as pl
from jax.experimental.pallas import tpu as pltpu
from jax.sharding import PartitionSpec as P

MESH = pl.DeviceIdType.MESH
HIGH = lax.Precision.HIGH

TB = 512
K = 256
RB = 4
CB = 4
SLOTS = 16
N_ROW = 8
N_COL = 16
CH = 4
SL = K // N_ROW

Z_PEERS = ((1, 0), (3, 0), (2, 0), (1, 1), (3, 1), (2, 1), (0, 1))
XY_PEERS = tuple(
    sorted(
        ((dx, dy) for dx in range(4) for dy in range(4) if dx or dy),
        key=lambda d: (min(d[0], 4 - d[0]) + min(d[1], 4 - d[1]), d),
    )
)


def kernel(
    tiles_hbm,
    q_hbm,
    p_hbm,
    coords,
    counts,
    row_partner,
    col_partner,
    out_ref,
    tiles,
    qin,
    pbuf,
    qt,
    ubuf,
    gv,
    kept,
    recv1_0,
    recv1_1,
    recv1_2,
    recv1_3,
    snd2,
    inc,
    cs,
    crecv_0,
    crecv_1,
    csnd2,
    cinc,
    cz1,
    cz1_in,
    cz2,
    cz2_in,
    slot_sm,
    live_sm,
    tile_sem,
    own_sem,
    q_own_sem,
    p_send,
    p_recv,
    q_send,
    q1_recv,
    q2_recv,
    q3_recv,
    s1_send,
    s1_recv,
    s2_send,
    s2_recv,
    x1_send,
    x1_recv,
    x2_send,
    x2_recv,
    c_send,
    c_recv,
):
    recv1 = (recv1_0, recv1_1, recv1_2, recv1_3)
    crecv = (crecv_0, crecv_1)
    r = lax.axis_index("row")
    c = lax.axis_index("col")
    z, core = r // 2, r % 2
    x, y = c // 4, c % 4

    z_peers = [((z + dz) % 4) * 2 + (core + dc) % 2 for dz, dc in Z_PEERS]
    xy_peers = [((x + dx) % 4) * 4 + (y + dy) % 4 for dx, dy in XY_PEERS]

    barrier = pltpu.get_barrier_semaphore()
    for peer in z_peers:
        pl.semaphore_signal(barrier, inc=1, device_id={"row": peer}, device_id_type=MESH)
    for peer in xy_peers:
        pl.semaphore_signal(barrier, inc=1, device_id={"col": peer}, device_id_type=MESH)

    own_cp = pltpu.make_async_copy(p_hbm, pbuf.at[z, core], own_sem)
    own_cp.start()
    q_cp = pltpu.make_async_copy(q_hbm, qin, q_own_sem)
    q_cp.start()
    tile_cp = pltpu.make_async_copy(tiles_hbm, tiles, tile_sem)
    tile_cp.start()

    q_cp.wait()
    qt[x, y] = qin[...].T
    own_cp.wait()

    def find_slot(pos, carry):
        slot = jnp.int32(0)
        for s in range(SLOTS):
            hit = coords[0, s] * CB + coords[1, s] == pos
            slot = jnp.where(hit, jnp.int32(s), slot)
        slot_sm[pos] = slot
        live_sm[pos] = jnp.where(slot < counts[0], jnp.int32(1), jnp.int32(0))
        return carry

    pl.semaphore_wait(barrier, len(z_peers) + len(xy_peers))

    up, down, far = lambda v: (v + 1) % 4, lambda v: (v + 3) % 4, lambda v: (v + 2) % 4
    hb = TB // 4
    sibling = z * 2 + (1 - core)

    p_cps = []

    def p_half(zs, cs_, h):
        return pbuf.at[zs, cs_, pl.ds(h * hb, hb)]

    def p_send_to(zs, h, row):
        n = len(p_cps)
        cp = pltpu.make_async_remote_copy(
            src_ref=p_half(zs, core, h),
            dst_ref=p_half(zs, core, h),
            send_sem=p_send.at[n],
            recv_sem=p_recv.at[zs, core, h],
            device_id={"row": row},
            device_id_type=MESH,
        )
        cp.start()
        p_cps.append(cp)

    def p_wait(zs, cs_, h):
        view = p_half(zs, cs_, h)
        pltpu.make_async_copy(view, view, p_recv.at[zs, cs_, h]).wait()

    z_up, z_down = up(z) * 2 + core, down(z) * 2 + core

    q_cps = []

    def q_ref_of(kind, i, j, lo, n):
        xs, ys = (i, j) if kind == 0 else (j, i)
        return qt.at[xs, ys, pl.ds(kind * 128 + lo, n)]

    me_i, me_j = (x, y), (y, x)

    def q_dest(kind, i, j):
        return i * 4 + j if kind == 0 else j * 4 + i

    def q_send_to(kind, i, j, lo, n, sem, dest):
        cp = pltpu.make_async_remote_copy(
            src_ref=q_ref_of(kind, i, j, lo, n),
            dst_ref=q_ref_of(kind, i, j, lo, n),
            send_sem=q_send.at[len(q_cps)],
            recv_sem=sem,
            device_id={"col": dest},
            device_id_type=MESH,
        )
        cp.start()
        q_cps.append(cp)

    def q_wait(kind, i, j, lo, n, sem):
        view = q_ref_of(kind, i, j, lo, n)
        pltpu.make_async_copy(view, view, sem).wait()

    def q_first(kind):
        i, j = me_i[kind], me_j[kind]
        for step in (up, down, far):
            q_send_to(kind, i, j, 0, 128, q1_recv.at[kind, i], q_dest(kind, step(i), j))

    def q_second(kind, i):
        mi, j = me_i[kind], me_j[kind]
        for step in (up, down):
            q_send_to(kind, i, j, 0, 128, q2_recv.at[kind, i, j], q_dest(kind, mi, step(j)))

    def q_take1(kind, step):
        i, j = step(me_i[kind]), me_j[kind]
        q_wait(kind, i, j, 0, 128, q1_recv.at[kind, i])
        q_second(kind, i)

    def q_take2(kind, i):
        mi, j = me_i[kind], me_j[kind]
        q_wait(kind, i, down(j), 0, 128, q2_recv.at[kind, i, down(j)])
        q_send_to(kind, i, down(j), 0, 64, q3_recv.at[kind, i, 0], q_dest(kind, mi, up(j)))
        q_wait(kind, i, up(j), 0, 128, q2_recv.at[kind, i, up(j)])
        q_send_to(kind, i, up(j), 64, 64, q3_recv.at[kind, i, 1], q_dest(kind, mi, down(j)))

    def q_take3(kind, i):
        j = far(me_j[kind])
        q_wait(kind, i, j, 0, 64, q3_recv.at[kind, i, 0])
        q_wait(kind, i, j, 64, 64, q3_recv.at[kind, i, 1])

    def apply_block(b):
        def one(a, carry):
            right = pbuf[b].reshape(TB, K)
            pos = a * CB + b
            tile = tiles[slot_sm[pos]]
            ubuf[pos] = jnp.dot(tile, right, precision=HIGH, preferred_element_type=jnp.float32)
            return carry

        lax.fori_loop(0, RB, one, 0)

    def apply_half(b, cs_, first):
        def one(a, carry):
            pos = a * CB + b
            cols = pl.ds(pl.multiple_of(cs_ * (TB // 2), TB // 2), TB // 2)
            tile = tiles[slot_sm[pos], :, cols]
            u = jnp.dot(tile, pbuf[b, cs_], precision=HIGH, preferred_element_type=jnp.float32)
            ubuf[pos] = u if first else ubuf[pos] + u
            return carry

        lax.fori_loop(0, RB, one, 0)

    for h in (0, 1):
        p_send_to(z, h, z_up)
        p_send_to(z, 1 - h, z_down)
    for kind in (0, 1):
        q_first(kind)
    for h in (0, 1):
        p_send_to(z, h, sibling)
    for kind in (0, 1):
        q_second(kind, me_i[kind])
    lax.fori_loop(0, RB * CB, find_slot, 0)
    for step in (up, down):
        for kind in (0, 1):
            q_take1(kind, step)
    for h in (0, 1):
        p_wait(z, 1 - core, h)
    tile_cp.wait()
    for kind in (0, 1):
        q_take1(kind, far)
    p_wait(down(z), core, 0)
    p_send_to(down(z), 0, z_up)
    p_wait(up(z), core, 1)
    p_send_to(up(z), 1, z_down)
    p_send_to(down(z), 0, sibling)
    p_send_to(up(z), 1, sibling)
    apply_block(z)
    for kind in (0, 1):
        q_take2(kind, me_i[kind])
    p_wait(down(z), core, 1)
    p_send_to(down(z), 1, sibling)
    p_wait(up(z), core, 0)
    p_send_to(up(z), 0, sibling)
    for step in (up, down):
        for kind in (0, 1):
            q_take2(kind, step(me_i[kind]))
    for h in (0, 1):
        p_wait(down(z), 1 - core, h)
    apply_block(down(z))
    for kind in (0, 1):
        q_take2(kind, far(me_i[kind]))
    for h in (0, 1):
        p_wait(far(z), core, h)
        p_send_to(far(z), h, sibling)
    for h in (0, 1):
        p_wait(up(z), 1 - core, h)
    apply_block(up(z))
    apply_half(far(z), core, True)
    for h in (0, 1):
        p_wait(far(z), 1 - core, h)
    apply_half(far(z), 1 - core, False)
    for kind in (0, 1):
        for step in (lambda v: v, up, down, far):
            q_take3(kind, step(me_i[kind]))

    my_rp = row_partner[r, c]
    my_cp = col_partner[r, c]
    my_h = jnp.where(r > my_rp, jnp.int32(1), jnp.int32(0))
    my_g = jnp.where(c > my_cp, jnp.int32(1), jnp.int32(0))
    partner_g = jnp.where(c > col_partner[my_rp, c], jnp.int32(1), jnp.int32(0))

    def blocks(dst, ch, row_half, keep_col):
        a = 2 * row_half + ch % 2
        col_half = (1 - keep_col) if ch < 2 else keep_col

        pos = a * CB + 2 * col_half
        left = jnp.concatenate([qt[a, i] for i in range(4)], axis=1)
        right = jnp.concatenate([ubuf[pos], ubuf[pos + 1]], axis=1)
        g = jnp.dot(left, right, precision=HIGH, preferred_element_type=jnp.float32)
        for n in range(2):
            gn = g[:, n * K : (n + 1) * K]
            gn = jnp.where(live_sm[pos + n] > 0, gn, jnp.zeros_like(gn))
            dst[ch, :, n] = gn.reshape(N_ROW, SL, K)

    def send1(ch):
        recv1[ch][r] = gv[ch, r]
        for peer in z_peers:
            pltpu.make_async_remote_copy(
                src_ref=gv.at[ch, peer],
                dst_ref=recv1[ch].at[r],
                send_sem=s1_send.at[ch],
                recv_sem=s1_recv.at[ch],
                device_id={"row": peer},
                device_id_type=MESH,
            ).start()

    def take(ref, n, sem):
        view = ref.at[pl.ds(0, n)]
        pltpu.make_async_copy(view, view, sem).wait()

    def row_send2(ch):
        inc[ch, r] = snd2[ch, r]
        for peer in z_peers:
            pltpu.make_async_remote_copy(
                src_ref=snd2.at[ch, peer],
                dst_ref=inc.at[ch, r],
                send_sem=s2_send.at[ch],
                recv_sem=s2_recv.at[ch],
                device_id={"row": peer},
                device_id_type=MESH,
            ).start()

    def send2(ch):
        take(recv1[ch], N_ROW - 1, s1_recv.at[ch])

        def one(k, carry):
            snd2[ch, k] = recv1[ch][row_partner[k, c]]
            return carry

        lax.fori_loop(0, N_ROW, one, 0)
        row_send2(ch)

    def cross1(ch):
        if ch == 0:
            cs[ch] = kept[ch].reshape(N_COL, SL, K)
        else:
            take(inc.at[ch], N_ROW - 1, s2_recv.at[ch])
            cs[ch] = (kept[ch] + inc[ch]).reshape(N_COL, SL, K)
        crecv[ch][c] = cs[ch, c]
        for peer in xy_peers:
            pltpu.make_async_remote_copy(
                src_ref=cs.at[ch, peer],
                dst_ref=crecv[ch].at[c],
                send_sem=x1_send.at[ch],
                recv_sem=x1_recv.at[ch],
                device_id={"col": peer},
                device_id_type=MESH,
            ).start()

    parts = [(m, slice(i * 8, i * 8 + 8), slice(j * 128, j * 128 + 128)) for m in range(2) for i in range(4) for j in range(2)]

    def slice_send(src, dst, n):
        dst[c] = src[c]
        for peer in xy_peers:
            pltpu.make_async_remote_copy(
                src_ref=src.at[peer],
                dst_ref=dst.at[c],
                send_sem=c_send.at[n],
                recv_sem=c_recv.at[n],
                device_id={"col": peer},
                device_id_type=MESH,
            ).start()

    def slices1():
        take(recv1[0], N_ROW - 1, s1_recv.at[0])

        def one(k, carry):
            value = recv1[0][row_partner[k, c]]
            for n, (m, rows, cols) in enumerate(parts):
                cz1[n, k] = value[m, rows, cols]
            return carry

        lax.fori_loop(0, N_ROW, one, 0)
        slice_send(cz1, cz1_in, 0)

    def slices2():
        take(cz1_in, N_COL - 1, c_recv.at[0])

        def one(n, carry):
            for k in range(N_ROW):
                cz2[n, k] = cz1_in[col_partner[k, n], k]
            return carry

        lax.fori_loop(0, N_COL, one, 0)
        slice_send(cz2, cz2_in, 1)

    def combine():
        take(cz2_in, N_COL - 1, c_recv.at[1])
        take(recv1[2], N_ROW - 1, s1_recv.at[2])

        def one(k, carry):
            value = recv1[2][row_partner[k, c]]
            for n, (m, rows, cols) in enumerate(parts):
                snd2[2, k, m, rows, cols] = value[m, rows, cols] + cz2_in[n, k]
            return carry

        lax.fori_loop(0, N_ROW, one, 0)
        row_send2(2)

    def cross2(ch):
        take(crecv[ch], N_COL - 1, x1_recv.at[ch])

        def one(k, carry):
            csnd2[ch, k] = crecv[ch][col_partner[r, k]]
            return carry

        lax.fori_loop(0, N_COL, one, 0)
        cinc[ch, c] = csnd2[ch, c]
        for peer in xy_peers:
            pltpu.make_async_remote_copy(
                src_ref=csnd2.at[ch, peer],
                dst_ref=cinc.at[ch, c],
                send_sem=x2_send.at[ch],
                recv_sem=x2_recv.at[ch],
                device_id={"col": peer},
                device_id_type=MESH,
            ).start()

    def finish(a):
        take(inc.at[2 + a], N_ROW - 1, s2_recv.at[2 + a])
        take(cinc.at[a], N_COL - 1, x2_recv.at[a])
        for n in range(2):
            total = kept[2 + a, :, n] + inc[2 + a, :, n]
            total = total + cinc[a].reshape(N_ROW, 2, SL, K)[:, n]
            out_ref[a * K : (a + 1) * K, n * K : (n + 1) * K] = total.reshape(K, K)

    given_h = 1 - my_h
    for ch in range(3):
        blocks(gv, ch, given_h, partner_g)
        send1(ch)
    blocks(kept, 0, my_h, my_g)
    cross1(0)
    blocks(gv, 3, given_h, partner_g)
    for ch in range(1, CH):
        blocks(kept, ch, my_h, my_g)
    slices1()
    send2(1)
    send1(3)
    cross2(0)
    slices2()
    cross1(1)
    combine()
    cross2(1)
    send2(3)
    finish(0)
    finish(1)

    for cp in p_cps + q_cps:
        cp.wait_send()
    for ch in range(CH):
        take(gv.at[ch], N_ROW - 1, s1_send.at[ch])
        if ch > 0:
            take(snd2.at[ch], N_ROW - 1, s2_send.at[ch])
    for ch in range(2):
        take(cs.at[ch], N_COL - 1, x1_send.at[ch])
        take(csnd2.at[ch], N_COL - 1, x2_send.at[ch])
        take((cz1, cz2)[ch], N_COL - 1, c_send.at[ch])


def body(tile_values, tile_coords, tile_counts, restrict_basis, prolong_basis, row_partner, col_partner):
    f32 = jnp.float32
    dma = pltpu.SemaphoreType.DMA
    any_spec = pl.BlockSpec(memory_space=pl.ANY)
    vmem_spec = pl.BlockSpec(memory_space=pltpu.VMEM)
    smem_spec = pl.BlockSpec(memory_space=pltpu.SMEM)
    return pl.pallas_call(
        kernel,
        out_shape=jax.ShapeDtypeStruct((RB * K // 2, CB * K // 2), f32),
        in_specs=[any_spec, any_spec, any_spec, smem_spec, smem_spec, smem_spec, smem_spec],
        out_specs=vmem_spec,
        scratch_shapes=[
            pltpu.VMEM((SLOTS, TB, TB), f32),
            pltpu.VMEM((TB // 4, K), f32),
            pltpu.VMEM((4, 2, TB // 2, K), f32),
            pltpu.VMEM((4, 4, K, TB // 4), f32),
            pltpu.VMEM((RB * CB, TB, K), f32),
            pltpu.VMEM((CH, N_ROW, 2, SL, K), f32),
            pltpu.VMEM((CH, N_ROW, 2, SL, K), f32),
            *[pltpu.VMEM((N_ROW, 2, SL, K), f32)] * CH,
            pltpu.VMEM((CH, N_ROW, 2, SL, K), f32),
            pltpu.VMEM((CH, N_ROW, 2, SL, K), f32),
            pltpu.VMEM((2, N_COL, SL, K), f32),
            *[pltpu.VMEM((N_COL, SL, K), f32)] * 2,
            pltpu.VMEM((2, N_COL, SL, K), f32),
            pltpu.VMEM((2, N_COL, SL, K), f32),
            *[pltpu.VMEM((N_COL, N_ROW, 8, 128), f32)] * 4,
            pltpu.SMEM((RB * CB,), jnp.int32),
            pltpu.SMEM((RB * CB,), jnp.int32),
            dma,
            dma,
            dma,
            dma((14,)),
            dma((4, 2, 2)),
            dma((38,)),
            dma((2, 4)),
            dma((2, 4, 4)),
            dma((2, 4, 2)),
            dma((CH,)),
            dma((CH,)),
            dma((CH,)),
            dma((CH,)),
            dma((2,)),
            dma((2,)),
            dma((2,)),
            dma((2,)),
            dma((2,)),
            dma((2,)),
        ],
        compiler_params=pltpu.CompilerParams(collective_id=0, has_side_effects=True, vmem_limit_bytes=60 << 20),
    )(tile_values, restrict_basis, prolong_basis, tile_coords.T, tile_counts, row_partner.T, col_partner)


def solution(mesh):
    in_specs = (
        P(("row", "col"), None, None),
        P(("row", "col"), None),
        P(("row", "col")),
        P(("row", "col"), None),
        P(("col", "row"), None),
        P(),
        P(),
    )
    return jax.shard_map(body, mesh=mesh, in_specs=in_specs, out_specs=P("row", "col"), check_vma=False)
```

```python
import jax
import jax.numpy as jnp
from jax import lax
from jax.experimental import pallas as pl
from jax.experimental.pallas import tpu as pltpu
from jax.sharding import PartitionSpec as P

MESH = pl.DeviceIdType.MESH
HIGH = lax.Precision.HIGH

TB = 512
K = 256
RB = 4
CB = 4
SLOTS = 16
N_ROW = 8
N_COL = 16
CH = 4
SL = K // N_ROW

Z_PEERS = ((1, 0), (3, 0), (2, 0), (1, 1), (3, 1), (2, 1), (0, 1))
XY_PEERS = tuple(
    sorted(
        ((dx, dy) for dx in range(4) for dy in range(4) if dx or dy),
        key=lambda d: (min(d[0], 4 - d[0]) + min(d[1], 4 - d[1]), d),
    )
)


def kernel(
    tiles_hbm,
    q_hbm,
    p_hbm,
    coords_hbm,
    counts_hbm,
    row_partner_hbm,
    col_partner_hbm,
    out_hbm,
    out_ref,
    tiles,
    qin,
    pbuf,
    qt,
    ubuf,
    gv,
    kept,
    recv1_0,
    recv1_1,
    recv1_2,
    recv1_3,
    snd2,
    inc,
    cs,
    crecv_0,
    crecv_1,
    csnd2,
    cinc,
    cz1,
    cz1_in,
    cz2,
    cz2_in,
    coords,
    counts,
    row_partner,
    col_partner,
    slot_sm,
    live_sm,
    table_sem,
    tile_sem,
    own_sem,
    q_own_sem,
    p_send,
    p_recv,
    q_send,
    q1_recv,
    q2_recv,
    s1_send,
    s1_recv,
    s2_send,
    s2_recv,
    x1_send,
    x1_recv,
    x2_send,
    x2_recv,
    out_sem,
    c_send,
    c_recv,
):
    recv1 = (recv1_0, recv1_1, recv1_2, recv1_3)
    crecv = (crecv_0, crecv_1)
    r = lax.axis_index("row")
    c = lax.axis_index("col")
    z, core = r // 2, r % 2
    x, y = c // 4, c % 4

    z_peers = [((z + dz) % 4) * 2 + (core + dc) % 2 for dz, dc in Z_PEERS]
    xy_peers = [((x + dx) % 4) * 4 + (y + dy) % 4 for dx, dy in XY_PEERS]

    barrier = pltpu.get_barrier_semaphore()
    for peer in z_peers:
        pl.semaphore_signal(barrier, inc=1, device_id={"row": peer}, device_id_type=MESH)
    for peer in xy_peers:
        pl.semaphore_signal(barrier, inc=1, device_id={"col": peer}, device_id_type=MESH)

    table_cps = []
    for ref, sm in (
        (coords_hbm, coords),
        (counts_hbm, counts),
        (row_partner_hbm, row_partner),
        (col_partner_hbm, col_partner),
    ):
        cp = pltpu.make_async_copy(ref, sm, table_sem.at[len(table_cps)])
        cp.start()
        table_cps.append(cp)
    own_cp = pltpu.make_async_copy(p_hbm, pbuf.at[z, core], own_sem)
    own_cp.start()
    q_cp = pltpu.make_async_copy(q_hbm, qin, q_own_sem)
    q_cp.start()
    tile_cp = pltpu.make_async_copy(tiles_hbm, tiles, tile_sem)
    tile_cp.start()

    q_cp.wait()
    qt[x, y] = qin[...].T
    own_cp.wait()

    def find_slot(pos, carry):
        slot = jnp.int32(0)
        for s in range(SLOTS):
            hit = coords[0, s] * CB + coords[1, s] == pos
            slot = jnp.where(hit, jnp.int32(s), slot)
        slot_sm[pos] = slot
        live_sm[pos] = jnp.where(slot < counts[0], jnp.int32(1), jnp.int32(0))
        return carry

    for cp in table_cps:
        cp.wait()
    lax.fori_loop(0, RB * CB, find_slot, 0)
    pl.semaphore_wait(barrier, len(z_peers) + len(xy_peers))

    up, down, far = lambda v: (v + 1) % 4, lambda v: (v + 3) % 4, lambda v: (v + 2) % 4
    hb = TB // 4
    sibling = z * 2 + (1 - core)

    p_cps = []

    def p_half(zs, cs_, h):
        return pbuf.at[zs, cs_, pl.ds(h * hb, hb)]

    def p_send_to(zs, h, row):
        n = len(p_cps)
        cp = pltpu.make_async_remote_copy(
            src_ref=p_half(zs, core, h),
            dst_ref=p_half(zs, core, h),
            send_sem=p_send.at[n],
            recv_sem=p_recv.at[zs, core, h],
            device_id={"row": row},
            device_id_type=MESH,
        )
        cp.start()
        p_cps.append(cp)

    def p_wait(zs, cs_, h):
        view = p_half(zs, cs_, h)
        pltpu.make_async_copy(view, view, p_recv.at[zs, cs_, h]).wait()

    z_up, z_down = up(z) * 2 + core, down(z) * 2 + core

    q_cps = []

    def q_ref_of(kind, i, j, lo, n):
        xs, ys = (i, j) if kind == 0 else (j, i)
        return qt.at[xs, ys, pl.ds(kind * 128 + lo, n)]

    me_i, me_j = (x, y), (y, x)

    def q_dest(kind, i, j):
        return i * 4 + j if kind == 0 else j * 4 + i

    def q_send_to(kind, i, j, lo, n, sem, dest):
        cp = pltpu.make_async_remote_copy(
            src_ref=q_ref_of(kind, i, j, lo, n),
            dst_ref=q_ref_of(kind, i, j, lo, n),
            send_sem=q_send.at[len(q_cps)],
            recv_sem=sem,
            device_id={"col": dest},
            device_id_type=MESH,
        )
        cp.start()
        q_cps.append(cp)

    def q_wait(kind, i, j, lo, n, sem):
        view = q_ref_of(kind, i, j, lo, n)
        pltpu.make_async_copy(view, view, sem).wait()

    def q_first(kind):
        i, j = me_i[kind], me_j[kind]
        for step in (up, down, far):
            q_send_to(kind, i, j, 0, 128, q1_recv.at[kind, i], q_dest(kind, step(i), j))

    def q_second(kind, i):
        mi, j = me_i[kind], me_j[kind]
        for step in (up, down, far):
            q_send_to(kind, i, j, 0, 128, q2_recv.at[kind, i, j], q_dest(kind, mi, step(j)))

    def q_take1(kind, step):
        i, j = step(me_i[kind]), me_j[kind]
        q_wait(kind, i, j, 0, 128, q1_recv.at[kind, i])
        q_second(kind, i)

    def q_take2(kind, i):
        for step in (up, down, far):
            j = step(me_j[kind])
            q_wait(kind, i, j, 0, 128, q2_recv.at[kind, i, j])

    def apply_block(b, lo=0, hi=RB):
        def one(a, carry):
            right = pbuf[b].reshape(TB, K)
            pos = a * CB + b
            tile = tiles[slot_sm[pos]]
            ubuf[pos] = jnp.dot(tile, right, precision=HIGH, preferred_element_type=jnp.float32)
            return carry

        lax.fori_loop(lo, hi, one, 0)

    def apply_half(b, cs_, first):
        def one(a, carry):
            pos = a * CB + b
            cols = pl.ds(pl.multiple_of(cs_ * (TB // 2), TB // 2), TB // 2)
            tile = tiles[slot_sm[pos], :, cols]
            u = jnp.dot(tile, pbuf[b, cs_], precision=HIGH, preferred_element_type=jnp.float32)
            ubuf[pos] = u if first else ubuf[pos] + u
            return carry

        lax.fori_loop(0, RB, one, 0)

    for h in (0, 1):
        p_send_to(z, h, z_up)
        p_send_to(z, 1 - h, z_down)
    for kind in (0, 1):
        q_first(kind)
    for h in (0, 1):
        p_send_to(z, h, sibling)
    for kind in (0, 1):
        q_second(kind, me_i[kind])
    for step in (up, down):
        for kind in (0, 1):
            q_take1(kind, step)
    for h in (0, 1):
        p_wait(z, 1 - core, h)
    tile_cp.wait()
    for kind in (0, 1):
        q_take1(kind, far)
    p_wait(down(z), core, 0)
    p_send_to(down(z), 0, z_up)
    p_wait(up(z), core, 1)
    p_send_to(up(z), 1, z_down)
    p_send_to(down(z), 0, sibling)
    p_send_to(up(z), 1, sibling)
    apply_block(z)
    p_wait(down(z), core, 1)
    p_send_to(down(z), 1, sibling)
    p_wait(up(z), core, 0)
    p_send_to(up(z), 0, sibling)
    for h in (0, 1):
        p_wait(down(z), 1 - core, h)
    apply_block(down(z))
    for h in (0, 1):
        p_wait(up(z), 1 - core, h)
    apply_block(up(z), 0, 1)
    for h in (0, 1):
        p_wait(far(z), core, h)
        p_send_to(far(z), h, sibling)
    apply_block(up(z), 1, RB)
    apply_half(far(z), core, True)
    for h in (0, 1):
        p_wait(far(z), 1 - core, h)
    apply_half(far(z), 1 - core, False)
    for kind in (0, 1):
        for step in (lambda v: v, up, down, far):
            q_take2(kind, step(me_i[kind]))

    my_rp = row_partner[r, c]
    my_cp = col_partner[r, c]
    my_h = jnp.where(r > my_rp, jnp.int32(1), jnp.int32(0))
    my_g = jnp.where(c > my_cp, jnp.int32(1), jnp.int32(0))
    partner_g = jnp.where(c > col_partner[my_rp, c], jnp.int32(1), jnp.int32(0))

    def blocks(dst, ch, row_half, keep_col):
        a = 2 * row_half + ch % 2
        col_half = (1 - keep_col) if ch < 2 else keep_col

        pos = a * CB + 2 * col_half
        left = jnp.concatenate([qt[a, i] for i in range(4)], axis=1)
        right = jnp.concatenate([ubuf[pos], ubuf[pos + 1]], axis=1)
        g = jnp.dot(left, right, precision=HIGH, preferred_element_type=jnp.float32)
        for n in range(2):
            gn = g[:, n * K : (n + 1) * K]
            gn = jnp.where(live_sm[pos + n] > 0, gn, jnp.zeros_like(gn))
            dst[ch, :, n] = gn.reshape(N_ROW, SL, K)

    def send1(ch):
        recv1[ch][r] = gv[ch, r]
        for peer in z_peers:
            pltpu.make_async_remote_copy(
                src_ref=gv.at[ch, peer],
                dst_ref=recv1[ch].at[r],
                send_sem=s1_send.at[ch],
                recv_sem=s1_recv.at[ch],
                device_id={"row": peer},
                device_id_type=MESH,
            ).start()

    def take(ref, n, sem):
        view = ref.at[pl.ds(0, n)]
        pltpu.make_async_copy(view, view, sem).wait()

    def row_send2(ch):
        inc[ch, r] = snd2[ch, r]
        for peer in z_peers:
            pltpu.make_async_remote_copy(
                src_ref=snd2.at[ch, peer],
                dst_ref=inc.at[ch, r],
                send_sem=s2_send.at[ch],
                recv_sem=s2_recv.at[ch],
                device_id={"row": peer},
                device_id_type=MESH,
            ).start()

    def send2(ch):
        take(recv1[ch], N_ROW - 1, s1_recv.at[ch])

        def one(k, carry):
            snd2[ch, k] = recv1[ch][row_partner[k, c]]
            return carry

        lax.fori_loop(0, N_ROW, one, 0)
        row_send2(ch)

    def cross1(ch):
        if ch == 0:
            cs[ch] = kept[ch].reshape(N_COL, SL, K)
        else:
            take(inc.at[ch], N_ROW - 1, s2_recv.at[ch])
            cs[ch] = (kept[ch] + inc[ch]).reshape(N_COL, SL, K)
        crecv[ch][c] = cs[ch, c]
        for peer in xy_peers:
            pltpu.make_async_remote_copy(
                src_ref=cs.at[ch, peer],
                dst_ref=crecv[ch].at[c],
                send_sem=x1_send.at[ch],
                recv_sem=x1_recv.at[ch],
                device_id={"col": peer},
                device_id_type=MESH,
            ).start()

    parts = [(m, slice(i * 8, i * 8 + 8), slice(j * 128, j * 128 + 128)) for m in range(2) for i in range(4) for j in range(2)]

    def slice_send(src, dst, n):
        dst[c] = src[c]
        for peer in xy_peers:
            pltpu.make_async_remote_copy(
                src_ref=src.at[peer],
                dst_ref=dst.at[c],
                send_sem=c_send.at[n],
                recv_sem=c_recv.at[n],
                device_id={"col": peer},
                device_id_type=MESH,
            ).start()

    def slices1():
        take(recv1[0], N_ROW - 1, s1_recv.at[0])

        def one(k, carry):
            value = recv1[0][row_partner[k, c]]
            for n, (m, rows, cols) in enumerate(parts):
                cz1[n, k] = value[m, rows, cols]
            return carry

        lax.fori_loop(0, N_ROW, one, 0)
        slice_send(cz1, cz1_in, 0)

    def slices2():
        take(cz1_in, N_COL - 1, c_recv.at[0])

        def one(n, carry):
            for k in range(N_ROW):
                cz2[n, k] = cz1_in[col_partner[k, n], k]
            return carry

        lax.fori_loop(0, N_COL, one, 0)
        slice_send(cz2, cz2_in, 1)

    def combine():
        take(cz2_in, N_COL - 1, c_recv.at[1])
        take(recv1[2], N_ROW - 1, s1_recv.at[2])

        def one(k, carry):
            value = recv1[2][row_partner[k, c]]
            for n, (m, rows, cols) in enumerate(parts):
                snd2[2, k, m, rows, cols] = value[m, rows, cols] + cz2_in[n, k]
            return carry

        lax.fori_loop(0, N_ROW, one, 0)
        row_send2(2)

    def cross2(ch):
        take(crecv[ch], N_COL - 1, x1_recv.at[ch])

        def one(k, carry):
            csnd2[ch, k] = crecv[ch][col_partner[r, k]]
            return carry

        lax.fori_loop(0, N_COL, one, 0)
        cinc[ch, c] = csnd2[ch, c]
        for peer in xy_peers:
            pltpu.make_async_remote_copy(
                src_ref=csnd2.at[ch, peer],
                dst_ref=cinc.at[ch, c],
                send_sem=x2_send.at[ch],
                recv_sem=x2_recv.at[ch],
                device_id={"col": peer},
                device_id_type=MESH,
            ).start()

    def finish(a):
        take(inc.at[2 + a], N_ROW - 1, s2_recv.at[2 + a])
        take(cinc.at[a], N_COL - 1, x2_recv.at[a])
        for n in range(2):
            total = kept[2 + a, :, n] + inc[2 + a, :, n]
            total = total + cinc[a].reshape(N_ROW, 2, SL, K)[:, n]
            out_ref[a * K : (a + 1) * K, n * K : (n + 1) * K] = total.reshape(K, K)
        rows = pl.ds(a * K, K)
        cp = pltpu.make_async_copy(out_ref.at[rows], out_hbm.at[rows], out_sem.at[a])
        cp.start()
        return cp

    given_h = 1 - my_h
    for ch in range(3):
        blocks(gv, ch, given_h, partner_g)
        send1(ch)
    blocks(kept, 0, my_h, my_g)
    cross1(0)
    blocks(gv, 3, given_h, partner_g)
    for ch in range(1, CH):
        blocks(kept, ch, my_h, my_g)
    slices1()
    send2(1)
    send1(3)
    cross2(0)
    slices2()
    cross1(1)
    combine()
    cross2(1)
    send2(3)
    out_cps = [finish(0), finish(1)]

    for cp in out_cps:
        cp.wait()
    for cp in p_cps + q_cps:
        cp.wait_send()
    for ch in range(CH):
        take(gv.at[ch], N_ROW - 1, s1_send.at[ch])
        if ch > 0:
            take(snd2.at[ch], N_ROW - 1, s2_send.at[ch])
    for ch in range(2):
        take(cs.at[ch], N_COL - 1, x1_send.at[ch])
        take(csnd2.at[ch], N_COL - 1, x2_send.at[ch])
        take((cz1, cz2)[ch], N_COL - 1, c_send.at[ch])


def body(tile_values, tile_coords, tile_counts, restrict_basis, prolong_basis, row_partner, col_partner):
    f32 = jnp.float32
    dma = pltpu.SemaphoreType.DMA
    any_spec = pl.BlockSpec(memory_space=pl.ANY)
    return pl.pallas_call(
        kernel,
        out_shape=jax.ShapeDtypeStruct((RB * K // 2, CB * K // 2), f32),
        in_specs=[any_spec] * 7,
        out_specs=any_spec,
        scratch_shapes=[
            pltpu.VMEM((RB * K // 2, CB * K // 2), f32),
            pltpu.VMEM((SLOTS, TB, TB), f32),
            pltpu.VMEM((TB // 4, K), f32),
            pltpu.VMEM((4, 2, TB // 2, K), f32),
            pltpu.VMEM((4, 4, K, TB // 4), f32),
            pltpu.VMEM((RB * CB, TB, K), f32),
            pltpu.VMEM((CH, N_ROW, 2, SL, K), f32),
            pltpu.VMEM((CH, N_ROW, 2, SL, K), f32),
            *[pltpu.VMEM((N_ROW, 2, SL, K), f32)] * CH,
            pltpu.VMEM((CH, N_ROW, 2, SL, K), f32),
            pltpu.VMEM((CH, N_ROW, 2, SL, K), f32),
            pltpu.VMEM((2, N_COL, SL, K), f32),
            *[pltpu.VMEM((N_COL, SL, K), f32)] * 2,
            pltpu.VMEM((2, N_COL, SL, K), f32),
            pltpu.VMEM((2, N_COL, SL, K), f32),
            *[pltpu.VMEM((N_COL, N_ROW, 8, 128), f32)] * 4,
            pltpu.SMEM((2, SLOTS), jnp.int32),
            pltpu.SMEM((1,), jnp.int32),
            pltpu.SMEM((N_ROW, N_COL), jnp.int32),
            pltpu.SMEM((N_ROW, N_COL), jnp.int32),
            pltpu.SMEM((RB * CB,), jnp.int32),
            pltpu.SMEM((RB * CB,), jnp.int32),
            dma((4,)),
            dma,
            dma,
            dma,
            dma((14,)),
            dma((4, 2, 2)),
            dma((30,)),
            dma((2, 4)),
            dma((2, 4, 4)),
            dma((CH,)),
            dma((CH,)),
            dma((CH,)),
            dma((CH,)),
            dma((2,)),
            dma((2,)),
            dma((2,)),
            dma((2,)),
            dma((2,)),
            dma((2,)),
            dma((2,)),
        ],
        compiler_params=pltpu.CompilerParams(collective_id=0, has_side_effects=True, vmem_limit_bytes=60 << 20),
    )(tile_values, restrict_basis, prolong_basis, tile_coords.T, tile_counts, row_partner.T, col_partner)


def solution(mesh):
    in_specs = (
        P(("row", "col"), None, None),
        P(("row", "col"), None),
        P(("row", "col")),
        P(("row", "col"), None),
        P(("col", "row"), None),
        P(),
        P(),
    )
    return jax.shard_map(body, mesh=mesh, in_specs=in_specs, out_specs=P("row", "col"), check_vma=False)
```

```python
import jax
import jax.numpy as jnp
from jax import lax
from jax.experimental import pallas as pl
from jax.experimental.pallas import tpu as pltpu
from jax.sharding import PartitionSpec as P

MESH = pl.DeviceIdType.MESH
HIGH = lax.Precision.HIGH

TB = 512
K = 256
RB = 4
CB = 4
SLOTS = 16
N_ROW = 8
N_COL = 16
CH = 4
SL = K // N_ROW

Z_PEERS = ((1, 0), (3, 0), (2, 0), (1, 1), (3, 1), (2, 1), (0, 1))
XY_PEERS = tuple(
    sorted(
        ((dx, dy) for dx in range(4) for dy in range(4) if dx or dy),
        key=lambda d: (min(d[0], 4 - d[0]) + min(d[1], 4 - d[1]), d),
    )
)


def kernel(
    tiles_hbm,
    q_hbm,
    p_hbm,
    coords_hbm,
    counts_hbm,
    row_partner_hbm,
    col_partner_hbm,
    out_ref,
    tiles,
    qin,
    pbuf,
    qt,
    ubuf,
    gv,
    kept,
    recv1_0,
    recv1_1,
    recv1_2,
    recv1_3,
    snd2,
    inc,
    cs,
    crecv_0,
    crecv_1,
    csnd2,
    cinc,
    cz1,
    cz1_in,
    cz2,
    cz2_in,
    coords,
    counts,
    row_partner,
    col_partner,
    slot_sm,
    live_sm,
    table_sem,
    tile_sem,
    own_sem,
    q_own_sem,
    p_send,
    p_recv,
    q_send,
    q1_recv,
    q2_recv,
    s1_send,
    s1_recv,
    s2_send,
    s2_recv,
    x1_send,
    x1_recv,
    x2_send,
    x2_recv,
    c_send,
    c_recv,
):
    recv1 = (recv1_0, recv1_1, recv1_2, recv1_3)
    crecv = (crecv_0, crecv_1)
    r = lax.axis_index("row")
    c = lax.axis_index("col")
    z, core = r // 2, r % 2
    x, y = c // 4, c % 4

    z_peers = [((z + dz) % 4) * 2 + (core + dc) % 2 for dz, dc in Z_PEERS]
    xy_peers = [((x + dx) % 4) * 4 + (y + dy) % 4 for dx, dy in XY_PEERS]

    barrier = pltpu.get_barrier_semaphore()
    for peer in z_peers:
        pl.semaphore_signal(barrier, inc=1, device_id={"row": peer}, device_id_type=MESH)
    for peer in xy_peers:
        pl.semaphore_signal(barrier, inc=1, device_id={"col": peer}, device_id_type=MESH)

    table_cps = []
    for ref, sm in (
        (coords_hbm, coords),
        (counts_hbm, counts),
        (row_partner_hbm, row_partner),
        (col_partner_hbm, col_partner),
    ):
        cp = pltpu.make_async_copy(ref, sm, table_sem.at[len(table_cps)])
        cp.start()
        table_cps.append(cp)
    own_cp = pltpu.make_async_copy(p_hbm, pbuf.at[z, core], own_sem)
    own_cp.start()
    q_cp = pltpu.make_async_copy(q_hbm, qin, q_own_sem)
    q_cp.start()
    tile_cp = pltpu.make_async_copy(tiles_hbm, tiles, tile_sem)
    tile_cp.start()

    q_cp.wait()
    qt[x, y] = qin[...].T
    own_cp.wait()

    def find_slot(pos, carry):
        slot = jnp.int32(0)
        for s in range(SLOTS):
            hit = coords[0, s] * CB + coords[1, s] == pos
            slot = jnp.where(hit, jnp.int32(s), slot)
        slot_sm[pos] = slot
        live_sm[pos] = jnp.where(slot < counts[0], jnp.int32(1), jnp.int32(0))
        return carry

    for cp in table_cps:
        cp.wait()
    lax.fori_loop(0, RB * CB, find_slot, 0)
    pl.semaphore_wait(barrier, len(z_peers) + len(xy_peers))

    up, down, far = lambda v: (v + 1) % 4, lambda v: (v + 3) % 4, lambda v: (v + 2) % 4
    hb = TB // 4
    sibling = z * 2 + (1 - core)

    p_cps = []

    def p_half(zs, cs_, h):
        return pbuf.at[zs, cs_, pl.ds(h * hb, hb)]

    def p_send_to(zs, h, row):
        n = len(p_cps)
        cp = pltpu.make_async_remote_copy(
            src_ref=p_half(zs, core, h),
            dst_ref=p_half(zs, core, h),
            send_sem=p_send.at[n],
            recv_sem=p_recv.at[zs, core, h],
            device_id={"row": row},
            device_id_type=MESH,
        )
        cp.start()
        p_cps.append(cp)

    def p_wait(zs, cs_, h):
        view = p_half(zs, cs_, h)
        pltpu.make_async_copy(view, view, p_recv.at[zs, cs_, h]).wait()

    z_up, z_down = up(z) * 2 + core, down(z) * 2 + core

    q_cps = []

    def q_ref_of(kind, i, j, lo, n):
        xs, ys = (i, j) if kind == 0 else (j, i)
        return qt.at[xs, ys, pl.ds(kind * 128 + lo, n)]

    me_i, me_j = (x, y), (y, x)

    def q_dest(kind, i, j):
        return i * 4 + j if kind == 0 else j * 4 + i

    def q_send_to(kind, i, j, lo, n, sem, dest):
        cp = pltpu.make_async_remote_copy(
            src_ref=q_ref_of(kind, i, j, lo, n),
            dst_ref=q_ref_of(kind, i, j, lo, n),
            send_sem=q_send.at[len(q_cps)],
            recv_sem=sem,
            device_id={"col": dest},
            device_id_type=MESH,
        )
        cp.start()
        q_cps.append(cp)

    def q_wait(kind, i, j, lo, n, sem):
        view = q_ref_of(kind, i, j, lo, n)
        pltpu.make_async_copy(view, view, sem).wait()

    def q_first(kind):
        i, j = me_i[kind], me_j[kind]
        for step in (up, down, far):
            q_send_to(kind, i, j, 0, 128, q1_recv.at[kind, i], q_dest(kind, step(i), j))

    def q_second(kind, i):
        mi, j = me_i[kind], me_j[kind]
        for step in (up, down, far):
            q_send_to(kind, i, j, 0, 128, q2_recv.at[kind, i, j], q_dest(kind, mi, step(j)))

    def q_take1(kind, step):
        i, j = step(me_i[kind]), me_j[kind]
        q_wait(kind, i, j, 0, 128, q1_recv.at[kind, i])
        q_second(kind, i)

    def q_take2(kind, i):
        for step in (up, down, far):
            j = step(me_j[kind])
            q_wait(kind, i, j, 0, 128, q2_recv.at[kind, i, j])

    def apply_block(b, lo=0, hi=RB):
        def one(a, carry):
            right = pbuf[b].reshape(TB, K)
            pos = a * CB + b
            tile = tiles[slot_sm[pos]]
            ubuf[pos] = jnp.dot(tile, right, precision=HIGH, preferred_element_type=jnp.float32)
            return carry

        lax.fori_loop(lo, hi, one, 0)

    def apply_half(b, cs_, first):
        def one(a, carry):
            pos = a * CB + b
            cols = pl.ds(pl.multiple_of(cs_ * (TB // 2), TB // 2), TB // 2)
            tile = tiles[slot_sm[pos], :, cols]
            u = jnp.dot(tile, pbuf[b, cs_], precision=HIGH, preferred_element_type=jnp.float32)
            ubuf[pos] = u if first else ubuf[pos] + u
            return carry

        lax.fori_loop(0, RB, one, 0)

    for h in (0, 1):
        p_send_to(z, h, z_up)
        p_send_to(z, 1 - h, z_down)
    for kind in (0, 1):
        q_first(kind)
    for h in (0, 1):
        p_send_to(z, h, sibling)
    for kind in (0, 1):
        q_second(kind, me_i[kind])
    for step in (up, down):
        for kind in (0, 1):
            q_take1(kind, step)
    for h in (0, 1):
        p_wait(z, 1 - core, h)
    tile_cp.wait()
    for kind in (0, 1):
        q_take1(kind, far)
    p_wait(down(z), core, 0)
    p_send_to(down(z), 0, z_up)
    p_wait(up(z), core, 1)
    p_send_to(up(z), 1, z_down)
    p_send_to(down(z), 0, sibling)
    p_send_to(up(z), 1, sibling)
    apply_block(z)
    p_wait(down(z), core, 1)
    p_send_to(down(z), 1, sibling)
    p_wait(up(z), core, 0)
    p_send_to(up(z), 0, sibling)
    for h in (0, 1):
        p_wait(down(z), 1 - core, h)
    apply_block(down(z))
    for h in (0, 1):
        p_wait(up(z), 1 - core, h)
    apply_block(up(z), 0, 1)
    for h in (0, 1):
        p_wait(far(z), core, h)
        p_send_to(far(z), h, sibling)
    apply_block(up(z), 1, RB)
    apply_half(far(z), core, True)
    for h in (0, 1):
        p_wait(far(z), 1 - core, h)
    apply_half(far(z), 1 - core, False)
    for kind in (0, 1):
        for step in (lambda v: v, up, down, far):
            q_take2(kind, step(me_i[kind]))

    my_rp = row_partner[r, c]
    my_cp = col_partner[r, c]
    my_h = jnp.where(r > my_rp, jnp.int32(1), jnp.int32(0))
    my_g = jnp.where(c > my_cp, jnp.int32(1), jnp.int32(0))
    partner_g = jnp.where(c > col_partner[my_rp, c], jnp.int32(1), jnp.int32(0))

    def blocks(dst, ch, row_half, keep_col):
        a = 2 * row_half + ch % 2
        col_half = (1 - keep_col) if ch < 2 else keep_col

        pos = a * CB + 2 * col_half
        left = jnp.concatenate([qt[a, i] for i in range(4)], axis=1)
        right = jnp.concatenate([ubuf[pos], ubuf[pos + 1]], axis=1)
        g = jnp.dot(left, right, precision=HIGH, preferred_element_type=jnp.float32)
        for n in range(2):
            gn = g[:, n * K : (n + 1) * K]
            gn = jnp.where(live_sm[pos + n] > 0, gn, jnp.zeros_like(gn))
            dst[ch, :, n] = gn.reshape(N_ROW, SL, K)

    def send1(ch):
        recv1[ch][r] = gv[ch, r]
        for peer in z_peers:
            pltpu.make_async_remote_copy(
                src_ref=gv.at[ch, peer],
                dst_ref=recv1[ch].at[r],
                send_sem=s1_send.at[ch],
                recv_sem=s1_recv.at[ch],
                device_id={"row": peer},
                device_id_type=MESH,
            ).start()

    def take(ref, n, sem):
        view = ref.at[pl.ds(0, n)]
        pltpu.make_async_copy(view, view, sem).wait()

    def row_send2(ch):
        inc[ch, r] = snd2[ch, r]
        for peer in z_peers:
            pltpu.make_async_remote_copy(
                src_ref=snd2.at[ch, peer],
                dst_ref=inc.at[ch, r],
                send_sem=s2_send.at[ch],
                recv_sem=s2_recv.at[ch],
                device_id={"row": peer},
                device_id_type=MESH,
            ).start()

    def send2(ch):
        take(recv1[ch], N_ROW - 1, s1_recv.at[ch])

        def one(k, carry):
            snd2[ch, k] = recv1[ch][row_partner[k, c]]
            return carry

        lax.fori_loop(0, N_ROW, one, 0)
        row_send2(ch)

    def cross1(ch):
        if ch == 0:
            cs[ch] = kept[ch].reshape(N_COL, SL, K)
        else:
            take(inc.at[ch], N_ROW - 1, s2_recv.at[ch])
            cs[ch] = (kept[ch] + inc[ch]).reshape(N_COL, SL, K)
        crecv[ch][c] = cs[ch, c]
        for peer in xy_peers:
            pltpu.make_async_remote_copy(
                src_ref=cs.at[ch, peer],
                dst_ref=crecv[ch].at[c],
                send_sem=x1_send.at[ch],
                recv_sem=x1_recv.at[ch],
                device_id={"col": peer},
                device_id_type=MESH,
            ).start()

    parts = [(m, slice(i * 8, i * 8 + 8), slice(j * 128, j * 128 + 128)) for m in range(2) for i in range(4) for j in range(2)]

    def slice_send(src, dst, n):
        dst[c] = src[c]
        for peer in xy_peers:
            pltpu.make_async_remote_copy(
                src_ref=src.at[peer],
                dst_ref=dst.at[c],
                send_sem=c_send.at[n],
                recv_sem=c_recv.at[n],
                device_id={"col": peer},
                device_id_type=MESH,
            ).start()

    def slices1():
        take(recv1[0], N_ROW - 1, s1_recv.at[0])

        def one(k, carry):
            value = recv1[0][row_partner[k, c]]
            for n, (m, rows, cols) in enumerate(parts):
                cz1[n, k] = value[m, rows, cols]
            return carry

        lax.fori_loop(0, N_ROW, one, 0)
        slice_send(cz1, cz1_in, 0)

    def slices2():
        take(cz1_in, N_COL - 1, c_recv.at[0])

        def one(n, carry):
            for k in range(N_ROW):
                cz2[n, k] = cz1_in[col_partner[k, n], k]
            return carry

        lax.fori_loop(0, N_COL, one, 0)
        slice_send(cz2, cz2_in, 1)

    def combine():
        take(cz2_in, N_COL - 1, c_recv.at[1])
        take(recv1[2], N_ROW - 1, s1_recv.at[2])

        def one(k, carry):
            value = recv1[2][row_partner[k, c]]
            for n, (m, rows, cols) in enumerate(parts):
                snd2[2, k, m, rows, cols] = value[m, rows, cols] + cz2_in[n, k]
            return carry

        lax.fori_loop(0, N_ROW, one, 0)
        row_send2(2)

    def cross2(ch):
        take(crecv[ch], N_COL - 1, x1_recv.at[ch])

        def one(k, carry):
            csnd2[ch, k] = crecv[ch][col_partner[r, k]]
            return carry

        lax.fori_loop(0, N_COL, one, 0)
        cinc[ch, c] = csnd2[ch, c]
        for peer in xy_peers:
            pltpu.make_async_remote_copy(
                src_ref=csnd2.at[ch, peer],
                dst_ref=cinc.at[ch, c],
                send_sem=x2_send.at[ch],
                recv_sem=x2_recv.at[ch],
                device_id={"col": peer},
                device_id_type=MESH,
            ).start()

    def finish(a):
        take(inc.at[2 + a], N_ROW - 1, s2_recv.at[2 + a])
        take(cinc.at[a], N_COL - 1, x2_recv.at[a])
        for n in range(2):
            total = kept[2 + a, :, n] + inc[2 + a, :, n]
            total = total + cinc[a].reshape(N_ROW, 2, SL, K)[:, n]
            out_ref[a * K : (a + 1) * K, n * K : (n + 1) * K] = total.reshape(K, K)

    given_h = 1 - my_h
    for ch in range(3):
        blocks(gv, ch, given_h, partner_g)
        send1(ch)
    blocks(kept, 0, my_h, my_g)
    cross1(0)
    blocks(gv, 3, given_h, partner_g)
    for ch in range(1, CH):
        blocks(kept, ch, my_h, my_g)
    slices1()
    send2(1)
    send1(3)
    cross2(0)
    slices2()
    cross1(1)
    combine()
    cross2(1)
    send2(3)
    finish(0)
    finish(1)

    for cp in p_cps + q_cps:
        cp.wait_send()
    for ch in range(CH):
        take(gv.at[ch], N_ROW - 1, s1_send.at[ch])
        if ch > 0:
            take(snd2.at[ch], N_ROW - 1, s2_send.at[ch])
    for ch in range(2):
        take(cs.at[ch], N_COL - 1, x1_send.at[ch])
        take(csnd2.at[ch], N_COL - 1, x2_send.at[ch])
        take((cz1, cz2)[ch], N_COL - 1, c_send.at[ch])


def body(tile_values, tile_coords, tile_counts, restrict_basis, prolong_basis, row_partner, col_partner):
    f32 = jnp.float32
    dma = pltpu.SemaphoreType.DMA
    return pl.pallas_call(
        kernel,
        out_shape=jax.ShapeDtypeStruct((RB * K // 2, CB * K // 2), f32),
        in_specs=[pl.BlockSpec(memory_space=pltpu.HBM)] * 4
        + [pl.BlockSpec(memory_space=pl.ANY)]
        + [pl.BlockSpec(memory_space=pltpu.HBM)] * 2,
        out_specs=pl.BlockSpec(memory_space=pltpu.VMEM),
        scratch_shapes=[
            pltpu.VMEM((SLOTS, TB, TB), f32),
            pltpu.VMEM((TB // 4, K), f32),
            pltpu.VMEM((4, 2, TB // 2, K), f32),
            pltpu.VMEM((4, 4, K, TB // 4), f32),
            pltpu.VMEM((RB * CB, TB, K), f32),
            pltpu.VMEM((CH, N_ROW, 2, SL, K), f32),
            pltpu.VMEM((CH, N_ROW, 2, SL, K), f32),
            *[pltpu.VMEM((N_ROW, 2, SL, K), f32)] * CH,
            pltpu.VMEM((CH, N_ROW, 2, SL, K), f32),
            pltpu.VMEM((CH, N_ROW, 2, SL, K), f32),
            pltpu.VMEM((2, N_COL, SL, K), f32),
            *[pltpu.VMEM((N_COL, SL, K), f32)] * 2,
            pltpu.VMEM((2, N_COL, SL, K), f32),
            pltpu.VMEM((2, N_COL, SL, K), f32),
            *[pltpu.VMEM((N_COL, N_ROW, 8, 128), f32)] * 4,
            pltpu.SMEM((2, SLOTS), jnp.int32),
            pltpu.SMEM((1,), jnp.int32),
            pltpu.SMEM((N_ROW, N_COL), jnp.int32),
            pltpu.SMEM((N_ROW, N_COL), jnp.int32),
            pltpu.SMEM((RB * CB,), jnp.int32),
            pltpu.SMEM((RB * CB,), jnp.int32),
            dma((4,)),
            dma,
            dma,
            dma,
            dma((14,)),
            dma((4, 2, 2)),
            dma((30,)),
            dma((2, 4)),
            dma((2, 4, 4)),
            dma((CH,)),
            dma((CH,)),
            dma((CH,)),
            dma((CH,)),
            dma((2,)),
            dma((2,)),
            dma((2,)),
            dma((2,)),
            dma((2,)),
            dma((2,)),
        ],
        compiler_params=pltpu.CompilerParams(collective_id=0, has_side_effects=True, vmem_limit_bytes=48 << 20),
    )(
        *[
            value if value.size == 1 else pltpu.with_memory_space_constraint(value, pltpu.HBM)
            for value in (
                tile_values,
                restrict_basis,
                prolong_basis,
                tile_coords.T,
                tile_counts,
                row_partner.T,
                col_partner,
            )
        ]
    )


def solution(mesh):
    in_specs = (
        P(("row", "col"), None, None),
        P(("row", "col"), None),
        P(("row", "col")),
        P(("row", "col"), None),
        P(("col", "row"), None),
        P(),
        P(),
    )
    return jax.shard_map(body, mesh=mesh, in_specs=in_specs, out_specs=P("row", "col"), check_vma=False)
```

```python
import jax
import jax.numpy as jnp
from jax import lax
from jax.experimental import pallas as pl
from jax.experimental.pallas import tpu as pltpu
from jax.sharding import PartitionSpec as P

MESH = pl.DeviceIdType.MESH
HIGH = lax.Precision.HIGH

TB = 512
K = 256
RB = 4
CB = 4
SLOTS = 16
N_ROW = 8
N_COL = 16
CH = 4
SL = K // N_ROW

Z_PEERS = ((1, 0), (3, 0), (2, 0), (1, 1), (3, 1), (2, 1), (0, 1))
XY_PEERS = tuple(
    sorted(
        ((dx, dy) for dx in range(4) for dy in range(4) if dx or dy),
        key=lambda d: (min(d[0], 4 - d[0]) + min(d[1], 4 - d[1]), d),
    )
)


def kernel(
    tiles_hbm,
    q_hbm,
    p_hbm,
    coords_hbm,
    counts_hbm,
    row_partner_hbm,
    col_partner_hbm,
    out_ref,
    tiles,
    qin,
    pbuf,
    qt,
    ubuf,
    gv,
    kept,
    recv1_0,
    recv1_1,
    recv1_2,
    recv1_3,
    snd2,
    inc,
    cs,
    crecv_0,
    crecv_1,
    csnd2,
    cinc,
    cz1,
    cz1_in,
    cz2,
    cz2_in,
    coords,
    counts,
    row_partner,
    col_partner,
    slot_sm,
    live_sm,
    table_sem,
    tile_sem,
    own_sem,
    q_own_sem,
    p_send,
    p_recv,
    q_send,
    q1_recv,
    q2_recv,
    s1_send,
    s1_recv,
    s2_send,
    s2_recv,
    x1_send,
    x1_recv,
    x2_send,
    x2_recv,
    c_send,
    c_recv,
):
    recv1 = (recv1_0, recv1_1, recv1_2, recv1_3)
    crecv = (crecv_0, crecv_1)
    r = lax.axis_index("row")
    c = lax.axis_index("col")
    z, core = r // 2, r % 2
    x, y = c // 4, c % 4

    z_peers = [((z + dz) % 4) * 2 + (core + dc) % 2 for dz, dc in Z_PEERS]
    xy_peers = [((x + dx) % 4) * 4 + (y + dy) % 4 for dx, dy in XY_PEERS]

    barrier = pltpu.get_barrier_semaphore()
    for peer in z_peers:
        pl.semaphore_signal(barrier, inc=1, device_id={"row": peer}, device_id_type=MESH)
    for peer in xy_peers:
        pl.semaphore_signal(barrier, inc=1, device_id={"col": peer}, device_id_type=MESH)

    table_cps = []
    for ref, sm in (
        (coords_hbm, coords),
        (counts_hbm, counts),
        (row_partner_hbm, row_partner),
        (col_partner_hbm, col_partner),
    ):
        cp = pltpu.make_async_copy(ref, sm, table_sem.at[len(table_cps)])
        cp.start()
        table_cps.append(cp)
    own_cp = pltpu.make_async_copy(p_hbm, pbuf.at[z, core], own_sem)
    own_cp.start()
    q_cp = pltpu.make_async_copy(q_hbm, qin, q_own_sem)
    q_cp.start()
    tile_cp = pltpu.make_async_copy(tiles_hbm, tiles, tile_sem)
    tile_cp.start()

    q_cp.wait()
    qt[x, y] = qin[...].T
    own_cp.wait()

    def find_slot(pos, carry):
        slot = jnp.int32(0)
        for s in range(SLOTS):
            hit = coords[0, s] * CB + coords[1, s] == pos
            slot = jnp.where(hit, jnp.int32(s), slot)
        slot_sm[pos] = slot
        live_sm[pos] = jnp.where(slot < counts[0], jnp.int32(1), jnp.int32(0))
        return carry

    for cp in table_cps:
        cp.wait()
    lax.fori_loop(0, RB * CB, find_slot, 0)
    pl.semaphore_wait(barrier, len(z_peers) + len(xy_peers))

    up, down, far = lambda v: (v + 1) % 4, lambda v: (v + 3) % 4, lambda v: (v + 2) % 4
    hb = TB // 4
    sibling = z * 2 + (1 - core)

    p_cps = []

    def p_half(zs, cs_, h):
        return pbuf.at[zs, cs_, pl.ds(h * hb, hb)]

    def p_send_to(zs, h, row):
        n = len(p_cps)
        cp = pltpu.make_async_remote_copy(
            src_ref=p_half(zs, core, h),
            dst_ref=p_half(zs, core, h),
            send_sem=p_send.at[n],
            recv_sem=p_recv.at[zs, core, h],
            device_id={"row": row},
            device_id_type=MESH,
        )
        cp.start()
        p_cps.append(cp)

    def p_wait(zs, cs_, h):
        view = p_half(zs, cs_, h)
        pltpu.make_async_copy(view, view, p_recv.at[zs, cs_, h]).wait()

    z_up, z_down = up(z) * 2 + core, down(z) * 2 + core

    q_cps = []

    def q_ref_of(kind, i, j, lo, n):
        xs, ys = (i, j) if kind == 0 else (j, i)
        return qt.at[xs, ys, pl.ds(kind * 128 + lo, n)]

    me_i, me_j = (x, y), (y, x)

    def q_dest(kind, i, j):
        return i * 4 + j if kind == 0 else j * 4 + i

    def q_send_to(kind, i, j, lo, n, sem, dest):
        cp = pltpu.make_async_remote_copy(
            src_ref=q_ref_of(kind, i, j, lo, n),
            dst_ref=q_ref_of(kind, i, j, lo, n),
            send_sem=q_send.at[len(q_cps)],
            recv_sem=sem,
            device_id={"col": dest},
            device_id_type=MESH,
        )
        cp.start()
        q_cps.append(cp)

    def q_wait(kind, i, j, lo, n, sem):
        view = q_ref_of(kind, i, j, lo, n)
        pltpu.make_async_copy(view, view, sem).wait()

    def q_first(kind):
        i, j = me_i[kind], me_j[kind]
        for step in (up, down, far):
            q_send_to(kind, i, j, 0, 128, q1_recv.at[kind, i], q_dest(kind, step(i), j))

    def q_second(kind, i):
        mi, j = me_i[kind], me_j[kind]
        for step in (up, down, far):
            q_send_to(kind, i, j, 0, 128, q2_recv.at[kind, i, j], q_dest(kind, mi, step(j)))

    def q_take1(kind, step):
        i, j = step(me_i[kind]), me_j[kind]
        q_wait(kind, i, j, 0, 128, q1_recv.at[kind, i])
        q_second(kind, i)

    def q_take2(kind, i):
        for step in (up, down, far):
            j = step(me_j[kind])
            q_wait(kind, i, j, 0, 128, q2_recv.at[kind, i, j])

    def apply_block(b, lo=0, hi=RB):
        def one(a, carry):
            right = pbuf[b].reshape(TB, K)
            pos = a * CB + b
            tile = tiles[slot_sm[pos]]
            ubuf[pos] = jnp.dot(tile, right, precision=HIGH, preferred_element_type=jnp.float32)
            return carry

        lax.fori_loop(lo, hi, one, 0)

    def apply_half(b, cs_, first):
        def one(a, carry):
            pos = a * CB + b
            cols = pl.ds(pl.multiple_of(cs_ * (TB // 2), TB // 2), TB // 2)
            tile = tiles[slot_sm[pos], :, cols]
            u = jnp.dot(tile, pbuf[b, cs_], precision=HIGH, preferred_element_type=jnp.float32)
            ubuf[pos] = u if first else ubuf[pos] + u
            return carry

        lax.fori_loop(0, RB, one, 0)

    for h in (0, 1):
        p_send_to(z, h, z_up)
        p_send_to(z, 1 - h, z_down)
    for kind in (0, 1):
        q_first(kind)
    for h in (0, 1):
        p_send_to(z, h, sibling)
    for kind in (0, 1):
        q_second(kind, me_i[kind])
    for step in (up, down):
        for kind in (0, 1):
            q_take1(kind, step)
    for h in (0, 1):
        p_wait(z, 1 - core, h)
    tile_cp.wait()
    for kind in (0, 1):
        q_take1(kind, far)
    p_wait(down(z), core, 0)
    p_send_to(down(z), 0, z_up)
    p_wait(up(z), core, 1)
    p_send_to(up(z), 1, z_down)
    p_send_to(down(z), 0, sibling)
    p_send_to(up(z), 1, sibling)
    apply_block(z)
    p_wait(down(z), core, 1)
    p_send_to(down(z), 1, sibling)
    p_wait(up(z), core, 0)
    p_send_to(up(z), 0, sibling)
    for h in (0, 1):
        p_wait(down(z), 1 - core, h)
    apply_block(down(z))
    for h in (0, 1):
        p_wait(up(z), 1 - core, h)
    apply_block(up(z), 0, 1)
    for h in (0, 1):
        p_wait(far(z), core, h)
        p_send_to(far(z), h, sibling)
    apply_block(up(z), 1, RB)
    apply_half(far(z), core, True)
    for h in (0, 1):
        p_wait(far(z), 1 - core, h)
    apply_half(far(z), 1 - core, False)
    for kind in (0, 1):
        for step in (lambda v: v, up, down, far):
            q_take2(kind, step(me_i[kind]))

    my_rp = row_partner[r, c]
    my_cp = col_partner[r, c]
    my_h = jnp.where(r > my_rp, jnp.int32(1), jnp.int32(0))
    my_g = jnp.where(c > my_cp, jnp.int32(1), jnp.int32(0))
    partner_g = jnp.where(c > col_partner[my_rp, c], jnp.int32(1), jnp.int32(0))

    def blocks(dst, ch, row_half, keep_col):
        a = 2 * row_half + ch % 2
        col_half = (1 - keep_col) if ch < 2 else keep_col

        pos = a * CB + 2 * col_half
        left = jnp.concatenate([qt[a, i] for i in range(4)], axis=1)
        right = jnp.concatenate([ubuf[pos], ubuf[pos + 1]], axis=1)
        g = jnp.dot(left, right, precision=HIGH, preferred_element_type=jnp.float32)
        for n in range(2):
            gn = g[:, n * K : (n + 1) * K]
            gn = jnp.where(live_sm[pos + n] > 0, gn, jnp.zeros_like(gn))
            dst[ch, :, n] = gn.reshape(N_ROW, SL, K)

    def send1(ch):
        recv1[ch][r] = gv[ch, r]
        for peer in z_peers:
            pltpu.make_async_remote_copy(
                src_ref=gv.at[ch, peer],
                dst_ref=recv1[ch].at[r],
                send_sem=s1_send.at[ch],
                recv_sem=s1_recv.at[ch],
                device_id={"row": peer},
                device_id_type=MESH,
            ).start()

    def take(ref, n, sem):
        view = ref.at[pl.ds(0, n)]
        pltpu.make_async_copy(view, view, sem).wait()

    def row_send2(ch):
        inc[ch, r] = snd2[ch, r]
        for peer in z_peers:
            pltpu.make_async_remote_copy(
                src_ref=snd2.at[ch, peer],
                dst_ref=inc.at[ch, r],
                send_sem=s2_send.at[ch],
                recv_sem=s2_recv.at[ch],
                device_id={"row": peer},
                device_id_type=MESH,
            ).start()

    def send2(ch):
        take(recv1[ch], N_ROW - 1, s1_recv.at[ch])

        def one(k, carry):
            snd2[ch, k] = recv1[ch][row_partner[k, c]]
            return carry

        lax.fori_loop(0, N_ROW, one, 0)
        row_send2(ch)

    def cross1(ch):
        if ch == 0:
            cs[ch] = kept[ch].reshape(N_COL, SL, K)
        else:
            take(inc.at[ch], N_ROW - 1, s2_recv.at[ch])
            cs[ch] = (kept[ch] + inc[ch]).reshape(N_COL, SL, K)
        crecv[ch][c] = cs[ch, c]
        for peer in xy_peers:
            pltpu.make_async_remote_copy(
                src_ref=cs.at[ch, peer],
                dst_ref=crecv[ch].at[c],
                send_sem=x1_send.at[ch],
                recv_sem=x1_recv.at[ch],
                device_id={"col": peer},
                device_id_type=MESH,
            ).start()

    parts = [(m, slice(i * 8, i * 8 + 8), slice(j * 128, j * 128 + 128)) for m in range(2) for i in range(4) for j in range(2)]

    def slice_send(src, dst, n):
        dst[c] = src[c]
        for peer in xy_peers:
            pltpu.make_async_remote_copy(
                src_ref=src.at[peer],
                dst_ref=dst.at[c],
                send_sem=c_send.at[n],
                recv_sem=c_recv.at[n],
                device_id={"col": peer},
                device_id_type=MESH,
            ).start()

    def slices1():
        take(recv1[0], N_ROW - 1, s1_recv.at[0])

        def one(k, carry):
            value = recv1[0][row_partner[k, c]]
            for n, (m, rows, cols) in enumerate(parts):
                cz1[n, k] = value[m, rows, cols]
            return carry

        lax.fori_loop(0, N_ROW, one, 0)
        slice_send(cz1, cz1_in, 0)

    def slices2():
        take(cz1_in, N_COL - 1, c_recv.at[0])

        def one(n, carry):
            for k in range(N_ROW):
                cz2[n, k] = cz1_in[col_partner[k, n], k]
            return carry

        lax.fori_loop(0, N_COL, one, 0)
        slice_send(cz2, cz2_in, 1)

    def combine():
        take(cz2_in, N_COL - 1, c_recv.at[1])
        take(recv1[2], N_ROW - 1, s1_recv.at[2])

        def one(k, carry):
            value = recv1[2][row_partner[k, c]]
            for n, (m, rows, cols) in enumerate(parts):
                snd2[2, k, m, rows, cols] = value[m, rows, cols] + cz2_in[n, k]
            return carry

        lax.fori_loop(0, N_ROW, one, 0)
        row_send2(2)

    def cross2(ch):
        take(crecv[ch], N_COL - 1, x1_recv.at[ch])

        def one(k, carry):
            csnd2[ch, k] = crecv[ch][col_partner[r, k]]
            return carry

        lax.fori_loop(0, N_COL, one, 0)
        cinc[ch, c] = csnd2[ch, c]
        for peer in xy_peers:
            pltpu.make_async_remote_copy(
                src_ref=csnd2.at[ch, peer],
                dst_ref=cinc.at[ch, c],
                send_sem=x2_send.at[ch],
                recv_sem=x2_recv.at[ch],
                device_id={"col": peer},
                device_id_type=MESH,
            ).start()

    def finish(a):
        take(inc.at[2 + a], N_ROW - 1, s2_recv.at[2 + a])
        take(cinc.at[a], N_COL - 1, x2_recv.at[a])
        for n in range(2):
            total = kept[2 + a, :, n] + inc[2 + a, :, n]
            total = total + cinc[a].reshape(N_ROW, 2, SL, K)[:, n]
            out_ref[a * K : (a + 1) * K, n * K : (n + 1) * K] = total.reshape(K, K)

    given_h = 1 - my_h
    for ch in range(3):
        blocks(gv, ch, given_h, partner_g)
        send1(ch)
    blocks(kept, 0, my_h, my_g)
    cross1(0)
    blocks(gv, 3, given_h, partner_g)
    for ch in range(1, CH):
        blocks(kept, ch, my_h, my_g)
    slices1()
    cross2(0)
    send2(1)
    send1(3)
    slices2()
    cross1(1)
    combine()
    cross2(1)
    send2(3)
    finish(0)
    finish(1)

    for cp in p_cps + q_cps:
        cp.wait_send()
    for ch in range(CH):
        take(gv.at[ch], N_ROW - 1, s1_send.at[ch])
        if ch > 0:
            take(snd2.at[ch], N_ROW - 1, s2_send.at[ch])
    for ch in range(2):
        take(cs.at[ch], N_COL - 1, x1_send.at[ch])
        take(csnd2.at[ch], N_COL - 1, x2_send.at[ch])
        take((cz1, cz2)[ch], N_COL - 1, c_send.at[ch])


def body(tile_values, tile_coords, tile_counts, restrict_basis, prolong_basis, row_partner, col_partner):
    f32 = jnp.float32
    dma = pltpu.SemaphoreType.DMA
    return pl.pallas_call(
        kernel,
        out_shape=jax.ShapeDtypeStruct((RB * K // 2, CB * K // 2), f32),
        in_specs=[pl.BlockSpec(memory_space=pltpu.HBM)] * 4
        + [pl.BlockSpec(memory_space=pl.ANY)]
        + [pl.BlockSpec(memory_space=pltpu.HBM)] * 2,
        out_specs=pl.BlockSpec(memory_space=pltpu.VMEM),
        scratch_shapes=[
            pltpu.VMEM((SLOTS, TB, TB), f32),
            pltpu.VMEM((TB // 4, K), f32),
            pltpu.VMEM((4, 2, TB // 2, K), f32),
            pltpu.VMEM((4, 4, K, TB // 4), f32),
            pltpu.VMEM((RB * CB, TB, K), f32),
            pltpu.VMEM((CH, N_ROW, 2, SL, K), f32),
            pltpu.VMEM((CH, N_ROW, 2, SL, K), f32),
            *[pltpu.VMEM((N_ROW, 2, SL, K), f32)] * CH,
            pltpu.VMEM((CH, N_ROW, 2, SL, K), f32),
            pltpu.VMEM((CH, N_ROW, 2, SL, K), f32),
            pltpu.VMEM((2, N_COL, SL, K), f32),
            *[pltpu.VMEM((N_COL, SL, K), f32)] * 2,
            pltpu.VMEM((2, N_COL, SL, K), f32),
            pltpu.VMEM((2, N_COL, SL, K), f32),
            *[pltpu.VMEM((N_COL, N_ROW, 8, 128), f32)] * 4,
            pltpu.SMEM((2, SLOTS), jnp.int32),
            pltpu.SMEM((1,), jnp.int32),
            pltpu.SMEM((N_ROW, N_COL), jnp.int32),
            pltpu.SMEM((N_ROW, N_COL), jnp.int32),
            pltpu.SMEM((RB * CB,), jnp.int32),
            pltpu.SMEM((RB * CB,), jnp.int32),
            dma((4,)),
            dma,
            dma,
            dma,
            dma((14,)),
            dma((4, 2, 2)),
            dma((30,)),
            dma((2, 4)),
            dma((2, 4, 4)),
            dma((CH,)),
            dma((CH,)),
            dma((CH,)),
            dma((CH,)),
            dma((2,)),
            dma((2,)),
            dma((2,)),
            dma((2,)),
            dma((2,)),
            dma((2,)),
        ],
        compiler_params=pltpu.CompilerParams(collective_id=0, has_side_effects=True, vmem_limit_bytes=48 << 20),
    )(
        *[
            value if value.size == 1 else pltpu.with_memory_space_constraint(value, pltpu.HBM)
            for value in (
                tile_values,
                restrict_basis,
                prolong_basis,
                tile_coords.T,
                tile_counts,
                row_partner.T,
                col_partner,
            )
        ]
    )


def solution(mesh):
    in_specs = (
        P(("row", "col"), None, None),
        P(("row", "col"), None),
        P(("row", "col")),
        P(("row", "col"), None),
        P(("col", "row"), None),
        P(),
        P(),
    )
    return jax.shard_map(body, mesh=mesh, in_specs=in_specs, out_specs=P("row", "col"), check_vma=False)
```
